32 devices in a mesh: ha: 4 (over z), wa: 4 (over y, x), head: 2 (over core).
Axes of the slice: x: 2, y: 2, z: 4, core: 2. Of those that a mesh axis runs over, the one named last changes fastest.
Arguments:
- queries: bfloat16 [64, 64, 3072], P('ha', 'wa', 'head'), may hold values from -5 to 5
- keys_values: bfloat16 [64, 64, 2, 3072], P('ha', 'wa', None, 'head'), may hold values from -5 to 5
- ref_cache: bfloat16 [8, 128, 2, 3072], P('wa', None, None, 'head'), may hold values from -5 to 5
- ref_ids: int32 [4, 4, 2], P('ha'), may hold values from 0 to 7, as said below
- flags: int32 [64, 64], P('ha', 'wa'), may hold values from 0 to 1, as said below
- proj_weight: bfloat16 [3072, 3072], P('head'), may hold values from -0.15625 to 0.15625
Outputs:
- projected: bfloat16 [64, 64, 3072], P('ha', 'wa', 'head')
The draws below stay inside these ranges and needn't reach their ends.
Inputs may be any that keep to these rules, and one draw needn't show every extreme that they name: `ref_ids`: the 2 ids of one tile give 2 different values of id // 2. `flags`: A tile of 16 x 16 tokens holds at most 64 flagged tokens, and some tile holds exactly 64.
All inputs are finite; a program needn't handle non-finite values.
Results may differ from the reference program's by a relative error of at most 0.0063.
Values may be sent and summed in bfloat16 or wider, within the bound.
No kernel may reach another device: no remote copies, remote signals or barrier semaphores. Data moves between devices by JAX's collectives and lax.ppermute only.
A program may use at most 128 MiB of HBM per device.

```python
import jax
import jax.numpy as jnp
from jax import lax

HEADS = 24
HD = 128
D = 3072
RADIUS = 16
TH = 16
TW = 16
GH = 64
GW = 64
RT = 128
REF_DEV = 2
NREF = 8
SEL = 2
FCAP = 64
N_HA = 4
N_WA = 4
N_HEAD = 2


def draw_queries(key, part):
    values = jax.random.normal(jax.random.fold_in(key, 11), (GH, GW, D), jnp.float32)
    return jnp.clip(values, -5.0, 5.0).astype(jnp.bfloat16)


def draw_keys_values(key, part):
    key_part = jax.random.normal(jax.random.fold_in(key, 21), (GH, GW, D), jnp.float32)
    value_part = jax.random.normal(jax.random.fold_in(key, 22), (GH, GW, D), jnp.float32)
    stacked = jnp.stack([key_part, value_part], axis=2)
    return jnp.clip(stacked, -5.0, 5.0).astype(jnp.bfloat16)


def draw_ref_ids(key, part):
    tile_count = N_HA * N_WA
    tile_keys = jax.random.split(jax.random.fold_in(key, 31), tile_count)
    owners = jax.vmap(lambda one_key: jax.random.permutation(one_key, N_WA)[:SEL])(tile_keys)
    slots = jax.random.randint(jax.random.fold_in(key, 32), (tile_count, SEL), 0, REF_DEV)
    return (owners * REF_DEV + slots).reshape(N_HA, N_WA, SEL).astype(jnp.int32)


def draw_flags(key, part):
    tile_count = N_HA * N_WA
    raw_count = jax.random.randint(jax.random.fold_in(key, 41), (tile_count,), 0, FCAP + 1)
    busiest = jax.random.randint(jax.random.fold_in(key, 42), (), 0, tile_count)
    raw_count = jnp.where(jnp.arange(tile_count) == busiest, FCAP, raw_count)
    counts = raw_count * raw_count // FCAP
    tile_keys = jax.random.split(jax.random.fold_in(key, 43), tile_count)
    orders = jax.vmap(lambda one_key: jax.random.permutation(one_key, TH * TW))(tile_keys)
    marked = (orders < counts[:, None]).astype(jnp.int32)
    return marked.reshape(N_HA, N_WA, TH, TW).transpose(0, 2, 1, 3).reshape(GH, GW)


def with_spikes(entries, rng, source, target, shards_of, factor):
    owner, partner = [(jnp.arange(entries.shape[position]) // (entries.shape[position] // shards_of)).reshape([-1 if axis == position else 1 for axis in range(entries.ndim)]) for position in (source, target)]
    chosen = jax.random.permutation(rng, shards_of)[partner]
    strong = (owner == chosen) | (owner == (partner + shards_of // 2) % shards_of)
    return jnp.where(strong, factor * entries, entries)


def level_of(rng, dims, cuts, smallest, largest):
    loudness, own = 1.0, jax.random.fold_in(rng, 6)
    for position, shards_of in cuts:
        steps = jnp.exp(jax.random.uniform(jax.random.fold_in(own, position), (shards_of,), jnp.float32, smallest / len(cuts), largest / len(cuts)))
        loudness = loudness * jnp.repeat(steps, dims[position] // shards_of).reshape([-1 if axis == position else 1 for axis in range(len(dims))])
    return loudness


def noise(own_key, dims, scale, limit, pieces=(), kind=jnp.bfloat16):
    values = scale * jax.random.normal(own_key, dims, jnp.float32)
    if pieces:
        values = values * level_of(own_key, dims, pieces, -0.22, 0.18)
    return jnp.clip(values, -limit, limit).astype(kind)


def bell_draw_with(rng, extent, scale, bound, pieces, heavy, kind=jnp.bfloat16):
    drawn = scale * jax.random.normal(rng, extent, jnp.float32)
    if pieces:
        drawn = drawn * level_of(rng, extent, pieces, -0.22, 0.18)
    return jnp.clip(with_spikes(drawn, jax.random.fold_in(rng, 3), *heavy), -bound, bound).astype(kind)


def setup_inputs(seed: int = 0) -> dict:
    key_list = jax.random.split(jax.random.key(seed), 7)
    queries = draw_queries(jax.random.fold_in(key_list[6], 71), 0)
    keys_values = draw_keys_values(jax.random.fold_in(key_list[6], 71), 0)
    ref_cache = noise(key_list[2], (NREF, RT, 2, D), 1.0, 5.0, ((0, 4), (3, 2)))
    ref_ids = draw_ref_ids(jax.random.fold_in(key_list[6], 71), 0)
    flags = draw_flags(jax.random.fold_in(key_list[6], 71), 0)
    proj_weight = bell_draw_with(key_list[5], (D, D), D ** -0.5, 0.15625, ((0, 2),), (0, 1, 2, 2.0))
    return dict(queries=queries, keys_values=keys_values, ref_cache=ref_cache, ref_ids=ref_ids, flags=flags, proj_weight=proj_weight)


def window_table():
    padded_rows = TH + 2 * RADIUS
    padded_cols = TW + 2 * RADIUS
    query_row = jnp.arange(TH)[:, None, None, None]
    query_col = jnp.arange(TW)[None, :, None, None]
    key_row = jnp.arange(padded_rows)[None, None, :, None]
    key_col = jnp.arange(padded_cols)[None, None, None, :]
    near = (jnp.abs(key_row - RADIUS - query_row) <= RADIUS) & (jnp.abs(key_col - RADIUS - query_col) <= RADIUS)
    return near.reshape(TH * TW, padded_rows * padded_cols)


def reference(queries, keys_values, ref_cache, ref_ids, flags, proj_weight):
    padded_rows = TH + 2 * RADIUS
    padded_cols = TW + 2 * RADIUS
    score_scale = HD ** -0.5
    padded_kv = jnp.pad(keys_values, ((RADIUS, RADIUS), (RADIUS, RADIUS), (0, 0), (0, 0)))
    inside = jnp.pad(jnp.ones((GH, GW), dtype=bool), RADIUS)
    near = window_table()
    weight_groups = proj_weight.astype(jnp.float32).reshape(N_HEAD, D // N_HEAD, D)
    anchor = jnp.zeros((), jnp.int32)

    def one_tile(tile_index):
        band = (tile_index // N_WA).astype(jnp.int32)
        lane = (tile_index % N_WA).astype(jnp.int32)
        row_start = (band * TH).astype(jnp.int32)
        col_start = (lane * TW).astype(jnp.int32)
        tile_query = lax.dynamic_slice(queries, (row_start, col_start, anchor), (TH, TW, D))
        tile_query = tile_query.reshape(TH * TW, HEADS, HD).astype(jnp.float32)
        tile_kv = lax.dynamic_slice(padded_kv, (row_start, col_start, anchor, anchor), (padded_rows, padded_cols, 2, D))
        tile_kv = tile_kv.reshape(padded_rows * padded_cols, 2, HEADS, HD).astype(jnp.float32)
        tile_inside = lax.dynamic_slice(inside, (row_start, col_start), (padded_rows, padded_cols)).reshape(-1)
        allowed = near & tile_inside[None, :]
        tile_flags = lax.dynamic_slice(flags, (row_start, col_start), (TH, TW)).reshape(-1) == 1
        chosen = ref_ids[band, lane]
        ref_block = jnp.take(ref_cache, chosen, axis=0).reshape(SEL * RT, 2, HEADS, HD).astype(jnp.float32)
        window_scores = jnp.einsum("qhc,khc->hqk", tile_query, tile_kv[:, 0]) * score_scale
        window_scores = jnp.where(allowed[None], window_scores, -jnp.inf)
        ref_scores = jnp.einsum("qhc,khc->hqk", tile_query, ref_block[:, 0]) * score_scale
        ref_scores = jnp.where(tile_flags[None, :, None], ref_scores, -jnp.inf)
        row_max = jnp.maximum(jnp.max(window_scores, axis=2), jnp.max(ref_scores, axis=2))
        window_probs = jnp.exp(window_scores - row_max[:, :, None])
        ref_probs = jnp.exp(ref_scores - row_max[:, :, None])
        denominator = jnp.sum(window_probs, axis=2) + jnp.sum(ref_probs, axis=2)
        window_soft = lax.optimization_barrier(window_probs.astype(jnp.bfloat16)).astype(jnp.float32)
        ref_soft = lax.optimization_barrier(ref_probs.astype(jnp.bfloat16)).astype(jnp.float32)
        numerator = jnp.einsum("hqk,khc->qhc", window_soft, tile_kv[:, 1]) + jnp.einsum("hqk,khc->qhc", ref_soft, ref_block[:, 1])
        attended = (numerator / jnp.transpose(denominator)[:, :, None]).reshape(TH * TW, D).astype(jnp.bfloat16)
        grouped = attended.astype(jnp.float32).reshape(TH * TW, N_HEAD, D // N_HEAD)
        partials = jnp.einsum("qgc,gcd->gqd", grouped, weight_groups)
        partials = lax.optimization_barrier(partials.astype(jnp.bfloat16)).astype(jnp.float32)
        return jnp.sum(partials, axis=0).astype(jnp.bfloat16).reshape(TH, TW, D)

    tiles = lax.map(one_tile, jnp.arange(N_HA * N_WA, dtype=jnp.int32))
    return tiles.reshape(N_HA, N_WA, TH, TW, D).transpose(0, 2, 1, 3, 4).reshape(GH, GW, D)
```

```python
import functools
import math

import jax
import jax.numpy as jnp
from jax import lax
from jax.experimental import pallas as pl
from jax.experimental.pallas import tpu as pltpu
from jax.sharding import PartitionSpec as P

HD = 128
RADIUS = 16
FAR = -131072.0


def extended(cells, sides, width):
    for axis, dim in sides:
        count = lax.axis_size(axis)
        ends = count - 1
        head = lax.slice_in_dim(cells, 0, width, axis=dim)
        tail = lax.slice_in_dim(cells, cells.shape[dim] - width, cells.shape[dim], axis=dim)
        cells = jnp.concatenate(
            [
                lax.ppermute(tail, axis, [(i, (i + 1) % count) for i in range(ends)]),
                cells,
                lax.ppermute(head, axis, [((i + 1) % count, i) for i in range(ends)]),
            ],
            axis=dim,
        )
    return cells


def by_tile(queries, keys_values, ref_cache, ref_ids, flags, proj_weight):
    tile_rows, tile_cols, channels = queries.shape
    head_count = channels // HD
    padded_rows = tile_rows + 2 * RADIUS
    padded_cols = tile_cols + 2 * RADIUS
    token_count = tile_rows * tile_cols
    score_scale = HD ** (-0.5)
    padded = extended(keys_values, (("ha", 0), ("wa", 1)), RADIUS)
    row_place = lax.axis_index("ha") * tile_rows - RADIUS + jnp.arange(padded_rows, dtype=jnp.int32)
    col_place = lax.axis_index("wa") * tile_cols - RADIUS + jnp.arange(padded_cols, dtype=jnp.int32)
    row_inside = (row_place >= 0) & (row_place < tile_rows * lax.axis_size("ha"))
    col_inside = (col_place >= 0) & (col_place < tile_cols * lax.axis_size("wa"))
    inside = row_inside[:, None] & col_inside[None, :]
    query_row = jnp.arange(tile_rows)[:, None, None, None]
    query_col = jnp.arange(tile_cols)[None, :, None, None]
    key_row = jnp.arange(padded_rows)[None, None, :, None]
    key_col = jnp.arange(padded_cols)[None, None, None, :]
    window = (jnp.abs(key_row - RADIUS - query_row) <= RADIUS) & (
        jnp.abs(key_col - RADIUS - query_col) <= RADIUS
    )
    window = (window & inside[None, None]).reshape(token_count, padded_rows * padded_cols)
    key_flat = padded[:, :, 0].reshape(padded_rows * padded_cols, channels)
    value_flat = padded[:, :, 1].reshape(padded_rows * padded_cols, channels)
    query_flat = queries.reshape(token_count, channels)
    flagged = flags.reshape(token_count) == 1
    wanted = ref_ids[0]
    my_blocks = lax.dynamic_index_in_dim(wanted, lax.axis_index("wa"), 0, keepdims=False)
    per_owner = ref_cache.shape[0]
    target = lax.axis_index("wa") * per_owner + jnp.arange(per_owner, dtype=jnp.int32)
    request_count = jnp.sum((wanted[:, :, None] == target[None, None, :]).astype(jnp.int32), axis=1)
    outgoing = jnp.einsum(
        "wr,rtkc->wtkc",
        request_count.astype(jnp.bfloat16),
        ref_cache,
        preferred_element_type=jnp.float32,
    ).astype(jnp.bfloat16)
    arrived = lax.all_to_all(outgoing, "wa", split_axis=0, concat_axis=0, tiled=True)
    picked = jnp.take(arrived, my_blocks // per_owner, axis=0)
    ref_keys = picked[:, :, 0].reshape(-1, channels)
    ref_values = picked[:, :, 1].reshape(-1, channels)
    head_outputs = []
    for head_index in range(head_count):
        first = head_index * HD
        head_query = query_flat[:, first : first + HD]
        scores = (
            jnp.einsum(
                "qc,kc->qk",
                head_query,
                key_flat[:, first : first + HD],
                preferred_element_type=jnp.float32,
            )
            * score_scale
        )
        scores = jnp.where(window, scores, -jnp.inf)
        row_max = jnp.max(scores, axis=1)
        ref_scores = (
            jnp.einsum(
                "qc,kc->qk",
                head_query,
                ref_keys[:, first : first + HD],
                preferred_element_type=jnp.float32,
            )
            * score_scale
        )
        ref_scores = jnp.where(flagged[:, None], ref_scores, -jnp.inf)
        row_max = jnp.maximum(row_max, jnp.max(ref_scores, axis=1))
        ref_probs = jnp.exp(ref_scores - row_max[:, None])
        ref_total = jnp.sum(ref_probs, axis=1)
        ref_part = jnp.dot(
            ref_probs.astype(jnp.bfloat16),
            ref_values[:, first : first + HD],
            preferred_element_type=jnp.float32,
        )
        probs = jnp.exp(scores - row_max[:, None])
        denominator = jnp.sum(probs, axis=1) + ref_total
        numerator = (
            jnp.dot(
                probs.astype(jnp.bfloat16),
                value_flat[:, first : first + HD],
                preferred_element_type=jnp.float32,
            )
            + ref_part
        )
        head_outputs.append(numerator / denominator[:, None])
    attended = jnp.concatenate(head_outputs, axis=1).astype(jnp.bfloat16)
    partial_term = jnp.dot(attended, proj_weight, preferred_element_type=jnp.float32).reshape(
        tile_rows, tile_cols, -1
    )
    return lax.psum_scatter(
        partial_term.astype(jnp.bfloat16), "head", scatter_dimension=2, tiled=True
    )


def attend_kernel(per_owner, ids_ref, q_ref, qf_ref, own_ref, up_ref, down_ref, ref_ref, kf_ref, o_ref, s_ref):
    tiles, token_count, _ = q_ref.shape
    block_tokens = ref_ref.shape[2] // per_owner
    chosen_count = ids_ref.shape[1]
    factor = HD ** (-0.5) * math.log2(math.e)
    ones = jnp.ones((token_count, HD), jnp.bfloat16)
    ones_block = jnp.ones((block_tokens, HD), jnp.bfloat16)
    for w in range(tiles):
        q_wide = jnp.concatenate([q_ref[w], qf_ref[w]], axis=1)
        window = []
        for other in range(max(w - 1, 0), min(w + 2, tiles)):
            for r, source in enumerate((up_ref, own_ref, down_ref)):
                window.append((source, other, r, other - w + 1))
        at = 0
        best = None
        spans = []

        def scored(keys, features, at, best):
            wide = jnp.concatenate([keys, features], axis=1)
            s = lax.dot_general(
                q_wide, wide, (((1,), (1,)), ((), ())), preferred_element_type=jnp.float32
            )
            width = s.shape[1]
            s_ref[:, at : at + width] = s
            for part in range(0, width, HD):
                piece = s[:, part : part + HD]
                best = piece if best is None else jnp.maximum(best, piece)
            return at + width, best

        for source, other, r, c in window:
            at, best = scored(source[other, 0], kf_ref[r, c], at, best)
        picks = []
        for n in range(chosen_count):
            chosen = ids_ref[w, n]
            owner = lax.div(chosen, per_owner)
            start = pl.multiple_of(lax.rem(chosen, per_owner) * block_tokens, block_tokens)
            picks.append((owner, start))
            at, best = scored(
                ref_ref[owner, 0, pl.ds(start, block_tokens)], kf_ref[3, 0, :block_tokens], at, best
            )
        row_max = jnp.max(best, axis=1, keepdims=True)
        at = 0
        total = jnp.zeros((token_count, 2 * HD), jnp.float32)

        def weighed(values, at, total):
            width = values.shape[0]
            probs = jnp.exp2((s_ref[:, at : at + width] - row_max) * factor)
            total = total + jnp.dot(
                probs.astype(jnp.bfloat16), values, preferred_element_type=jnp.float32
            )
            return at + width, total

        for source, other, r, c in window:
            at, total = weighed(jnp.concatenate([source[other, 1], ones], axis=1), at, total)
        for owner, start in picks:
            at, total = weighed(
                jnp.concatenate([ref_ref[owner, 1, pl.ds(start, block_tokens)], ones_block], axis=1),
                at,
                total,
            )
        o_ref[w] = (total[:, :HD] / total[:, HD:]).astype(jnp.bfloat16)


def attend(per_owner, ids, q, q_features, own, up, down, ref, k_features):
    tiles, token_count, _ = q.shape
    key_count = 9 * token_count + ids.shape[1] * (ref.shape[2] // per_owner)
    vmem = pl.BlockSpec(memory_space=pltpu.VMEM)
    return pl.pallas_call(
        functools.partial(attend_kernel, per_owner),
        out_shape=jax.ShapeDtypeStruct(q.shape, jnp.bfloat16),
        in_specs=[pl.BlockSpec(memory_space=pltpu.SMEM)] + [vmem] * 7,
        out_specs=vmem,
        scratch_shapes=[pltpu.VMEM((token_count, key_count), jnp.float32)],
        compiler_params=pltpu.CompilerParams(vmem_limit_bytes=40 << 20),
        name="attend",
    )(ids, q, q_features, own, up, down, ref, k_features)


def features(tile_rows, tile_cols, flags):
    token_count = tile_rows * tile_cols
    lane = lax.broadcasted_iota(jnp.int32, (token_count, HD), 1)
    token = lax.broadcasted_iota(jnp.int32, (token_count, HD), 0)
    row, col = token // tile_cols, token % tile_cols
    row_lane = lane
    col_lane = lane - tile_rows
    is_row = lane < tile_rows
    is_col = (lane >= tile_rows) & (lane < tile_rows + tile_cols)
    is_flag = lane == tile_rows + tile_cols
    hot = (is_row & (row_lane == row)) | (is_col & (col_lane == col))
    q_features = jnp.where(
        is_flag[None], (1 - flags)[:, :, None], hot.astype(jnp.int32)[None]
    ).astype(jnp.bfloat16)
    place = lax.axis_index("ha")
    last = lax.axis_size("ha") - 1
    row_far = [
        is_row & ((row < row_lane) | (place == 0)),
        jnp.zeros_like(is_row),
        is_row & ((row > row_lane) | (place == last)),
    ]
    col_far = [is_col & (col < col_lane), jnp.zeros_like(is_col), is_col & (col > col_lane)]
    zero = jnp.zeros_like(is_row)
    table = [[row_far[r] | col_far[c] for c in range(3)] for r in range(3)] + [[is_flag, zero, zero]]
    k_features = jnp.where(jnp.array(0) == 0, jnp.stack([jnp.stack(t) for t in table]), False)
    return q_features, jnp.where(k_features, FAR, 0.0).astype(jnp.bfloat16)


def by_head(queries, keys_values, ref_cache, ref_ids, flags, proj_weight):
    tile_rows, tile_cols, channels = queries.shape
    tiles = lax.axis_size("wa")
    token_count = tile_rows * tile_cols
    share = channels // HD // tiles
    per_owner, block_tokens = ref_cache.shape[:2]
    heights = lax.axis_size("ha")
    kv = keys_values.reshape(token_count, 2, tiles, share, HD)
    qs = queries.reshape(token_count, tiles, share, HD)
    rc = ref_cache.reshape(per_owner * block_tokens, 2, tiles, share, HD)

    def swap(x):
        return lax.all_to_all(x, "wa", split_axis=0, concat_axis=0, tiled=True)

    down_pairs = [(i, i + 1) for i in range(heights - 1)]
    up_pairs = [(i + 1, i) for i in range(heights - 1)]
    all_flags = lax.all_gather(flags.reshape(token_count), "wa", axis=0)
    q_features, k_features = features(tile_rows, tile_cols, all_flags)
    outs = []
    for n in range(share):
        own = swap(kv[:, :, :, n].transpose(2, 1, 0, 3))
        up = lax.ppermute(own, "ha", down_pairs)
        down = lax.ppermute(own, "ha", up_pairs)
        q = swap(qs[:, :, n].transpose(1, 0, 2))
        ref = swap(rc[:, :, :, n].transpose(2, 1, 0, 3))
        out = attend(per_owner, ref_ids[0], q, q_features, own, up, down, ref, k_features)
        outs.append(swap(out))
    attended = jnp.stack(outs, axis=1).transpose(2, 0, 1, 3).reshape(token_count, channels)
    half = proj_weight.shape[1] // 2
    mine = lax.axis_index("head")
    theirs = 1 - mine

    def partial(which):
        columns = lax.dynamic_slice_in_dim(proj_weight, which * half, half, 1)
        return jnp.dot(attended, columns, preferred_element_type=jnp.float32).astype(jnp.bfloat16)

    arrived = lax.ppermute(partial(theirs), "head", [(0, 1), (1, 0)])
    total = partial(mine).astype(jnp.float32) + arrived.astype(jnp.float32)
    return total.astype(jnp.bfloat16).reshape(tile_rows, tile_cols, half)


def on_device(queries, *others):
    head_count = queries.shape[2] // HD
    fits = (
        head_count % lax.axis_size("wa") == 0
        and lax.axis_size("head") == 2
        and queries.shape[0] == RADIUS
        and queries.shape[1] == RADIUS
    )
    return (by_head if fits else by_tile)(queries, *others)


def solution(mesh):
    return jax.shard_map(
        on_device,
        mesh=mesh,
        in_specs=(
            P("ha", "wa", "head"),
            P("ha", "wa", None, "head"),
            P("wa", None, None, "head"),
            P("ha", None, None),
            P("ha", "wa"),
            P("head", None),
        ),
        out_specs=P("ha", "wa", "head"),
        check_vma=False,
    )
```

```python
import functools
import math

import jax
import jax.numpy as jnp
from jax import lax
from jax.experimental import pallas as pl
from jax.experimental.pallas import tpu as pltpu
from jax.sharding import PartitionSpec as P

HD = 128
RADIUS = 16
FAR = -131072.0


def extended(cells, sides, width):
    for axis, dim in sides:
        count = lax.axis_size(axis)
        ends = count - 1
        head = lax.slice_in_dim(cells, 0, width, axis=dim)
        tail = lax.slice_in_dim(cells, cells.shape[dim] - width, cells.shape[dim], axis=dim)
        cells = jnp.concatenate(
            [
                lax.ppermute(tail, axis, [(i, (i + 1) % count) for i in range(ends)]),
                cells,
                lax.ppermute(head, axis, [((i + 1) % count, i) for i in range(ends)]),
            ],
            axis=dim,
        )
    return cells


def by_tile(queries, keys_values, ref_cache, ref_ids, flags, proj_weight):
    tile_rows, tile_cols, channels = queries.shape
    head_count = channels // HD
    padded_rows = tile_rows + 2 * RADIUS
    padded_cols = tile_cols + 2 * RADIUS
    token_count = tile_rows * tile_cols
    score_scale = HD ** (-0.5)
    padded = extended(keys_values, (("ha", 0), ("wa", 1)), RADIUS)
    row_place = lax.axis_index("ha") * tile_rows - RADIUS + jnp.arange(padded_rows, dtype=jnp.int32)
    col_place = lax.axis_index("wa") * tile_cols - RADIUS + jnp.arange(padded_cols, dtype=jnp.int32)
    row_inside = (row_place >= 0) & (row_place < tile_rows * lax.axis_size("ha"))
    col_inside = (col_place >= 0) & (col_place < tile_cols * lax.axis_size("wa"))
    inside = row_inside[:, None] & col_inside[None, :]
    query_row = jnp.arange(tile_rows)[:, None, None, None]
    query_col = jnp.arange(tile_cols)[None, :, None, None]
    key_row = jnp.arange(padded_rows)[None, None, :, None]
    key_col = jnp.arange(padded_cols)[None, None, None, :]
    window = (jnp.abs(key_row - RADIUS - query_row) <= RADIUS) & (
        jnp.abs(key_col - RADIUS - query_col) <= RADIUS
    )
    window = (window & inside[None, None]).reshape(token_count, padded_rows * padded_cols)
    key_flat = padded[:, :, 0].reshape(padded_rows * padded_cols, channels)
    value_flat = padded[:, :, 1].reshape(padded_rows * padded_cols, channels)
    query_flat = queries.reshape(token_count, channels)
    flagged = flags.reshape(token_count) == 1
    wanted = ref_ids[0]
    my_blocks = lax.dynamic_index_in_dim(wanted, lax.axis_index("wa"), 0, keepdims=False)
    per_owner = ref_cache.shape[0]
    target = lax.axis_index("wa") * per_owner + jnp.arange(per_owner, dtype=jnp.int32)
    request_count = jnp.sum((wanted[:, :, None] == target[None, None, :]).astype(jnp.int32), axis=1)
    outgoing = jnp.einsum(
        "wr,rtkc->wtkc",
        request_count.astype(jnp.bfloat16),
        ref_cache,
        preferred_element_type=jnp.float32,
    ).astype(jnp.bfloat16)
    arrived = lax.all_to_all(outgoing, "wa", split_axis=0, concat_axis=0, tiled=True)
    picked = jnp.take(arrived, my_blocks // per_owner, axis=0)
    ref_keys = picked[:, :, 0].reshape(-1, channels)
    ref_values = picked[:, :, 1].reshape(-1, channels)
    head_outputs = []
    for head_index in range(head_count):
        first = head_index * HD
        head_query = query_flat[:, first : first + HD]
        scores = (
            jnp.einsum(
                "qc,kc->qk",
                head_query,
                key_flat[:, first : first + HD],
                preferred_element_type=jnp.float32,
            )
            * score_scale
        )
        scores = jnp.where(window, scores, -jnp.inf)
        row_max = jnp.max(scores, axis=1)
        ref_scores = (
            jnp.einsum(
                "qc,kc->qk",
                head_query,
                ref_keys[:, first : first + HD],
                preferred_element_type=jnp.float32,
            )
            * score_scale
        )
        ref_scores = jnp.where(flagged[:, None], ref_scores, -jnp.inf)
        row_max = jnp.maximum(row_max, jnp.max(ref_scores, axis=1))
        ref_probs = jnp.exp(ref_scores - row_max[:, None])
        ref_total = jnp.sum(ref_probs, axis=1)
        ref_part = jnp.dot(
            ref_probs.astype(jnp.bfloat16),
            ref_values[:, first : first + HD],
            preferred_element_type=jnp.float32,
        )
        probs = jnp.exp(scores - row_max[:, None])
        denominator = jnp.sum(probs, axis=1) + ref_total
        numerator = (
            jnp.dot(
                probs.astype(jnp.bfloat16),
                value_flat[:, first : first + HD],
                preferred_element_type=jnp.float32,
            )
            + ref_part
        )
        head_outputs.append(numerator / denominator[:, None])
    attended = jnp.concatenate(head_outputs, axis=1).astype(jnp.bfloat16)
    partial_term = jnp.dot(attended, proj_weight, preferred_element_type=jnp.float32).reshape(
        tile_rows, tile_cols, -1
    )
    return lax.psum_scatter(
        partial_term.astype(jnp.bfloat16), "head", scatter_dimension=2, tiled=True
    )


VMEM = pl.BlockSpec(memory_space=pltpu.VMEM)
SMEM = pl.BlockSpec(memory_space=pltpu.SMEM)
ANY = pl.BlockSpec(memory_space=pl.ANY)


def copied(pairs, sem):
    copies = [
        pltpu.make_async_copy(source, target, sem.at[n]) for n, (source, target) in enumerate(pairs)
    ]
    for copy in copies:
        copy.start()
    for copy in copies:
        copy.wait()


def attend_kernel(per_owner, tiles, count, me_ref, ids_ref, *refs):
    come, (qf_ref, own_ref, a_ref, b_ref, kf_ref) = refs[:tiles], refs[tiles : tiles + 5]
    o_refs, scratch = refs[tiles + 5 : 2 * tiles + 5], refs[2 * tiles + 5 :]
    s_ref, qr_ref, out_ref = scratch
    token_count = qf_ref.shape[1]
    head_rows = qr_ref.shape[1] // count
    block_tokens = (head_rows - token_count) // 2 // per_owner
    chosen_count = ids_ref.shape[1]
    factor = HD ** (-0.5) * math.log2(math.e)
    ones = jnp.ones((token_count, HD), jnp.bfloat16)
    ones_block = jnp.ones((block_tokens, HD), jnp.bfloat16)
    for k in range(tiles):
        qr_ref[me_ref[0] ^ k] = come[k][: qr_ref.shape[1]]
    for head in range(count):
        query_at = head * head_rows
        key_at = query_at + token_count
        value_at = key_at + per_owner * block_tokens
        for w in range(tiles):
            queries = qr_ref[w, query_at : query_at + token_count]
            q_wide = jnp.concatenate([queries, qf_ref[w]], axis=1)
            window = []
            for other in range(max(w - 1, 0), min(w + 2, tiles)):
                for r, source in enumerate((a_ref, own_ref, b_ref)):
                    window.append((source, other, r, other - w + 1))
            at = 0
            best = None

            def scored(keys, features, at, best):
                wide = jnp.concatenate([keys, features], axis=1)
                s = lax.dot_general(
                    q_wide, wide, (((1,), (1,)), ((), ())), preferred_element_type=jnp.float32
                )
                width = s.shape[1]
                s_ref[:, at : at + width] = s
                for part in range(0, width, HD):
                    piece = s[:, part : part + HD]
                    best = piece if best is None else jnp.maximum(best, piece)
                return at + width, best

            for source, other, r, c in window:
                at, best = scored(source[other, 2 * head], kf_ref[r, c], at, best)
            picks = []
            for n in range(chosen_count):
                chosen = ids_ref[w, n]
                owner = lax.div(chosen, per_owner)
                start = pl.multiple_of(lax.rem(chosen, per_owner) * block_tokens, block_tokens)
                picks.append((owner, start))
                at, best = scored(
                    qr_ref[owner, pl.ds(key_at + start, block_tokens)],
                    kf_ref[3, 0, :block_tokens],
                    at,
                    best,
                )
            row_max = jnp.max(best, axis=1, keepdims=True)
            at = 0
            total = jnp.zeros((token_count, 2 * HD), jnp.float32)

            def weighed(values, at, total):
                width = values.shape[0]
                probs = jnp.exp2((s_ref[:, at : at + width] - row_max) * factor)
                total = total + jnp.dot(
                    probs.astype(jnp.bfloat16), values, preferred_element_type=jnp.float32
                )
                return at + width, total

            for source, other, r, c in window:
                values = source[other, 2 * head + 1]
                at, total = weighed(jnp.concatenate([values, ones], axis=1), at, total)
            for owner, start in picks:
                values = qr_ref[owner, pl.ds(value_at + start, block_tokens)]
                at, total = weighed(jnp.concatenate([values, ones_block], axis=1), at, total)
            out_ref[w, head * token_count : (head + 1) * token_count] = (
                total[:, :HD] / total[:, HD:]
            ).astype(jnp.bfloat16)
    for k in range(tiles):
        o_refs[k][...] = out_ref[me_ref[0] ^ k]


def attend(per_owner, me, ids, qr, q_features, own, first, second, k_features):
    tiles, token_count, _ = q_features.shape
    count = own.shape[1] // 2
    key_count = (9 + ids.shape[1]) * token_count
    rows = qr[0].shape[0] // 128 * 128
    return pl.pallas_call(
        functools.partial(attend_kernel, per_owner, tiles, count),
        out_shape=[jax.ShapeDtypeStruct((count * token_count, HD), jnp.bfloat16)] * tiles,
        in_specs=[SMEM] * 2 + [VMEM] * (tiles + 5),
        out_specs=[VMEM] * tiles,
        scratch_shapes=[
            pltpu.VMEM((token_count, key_count), jnp.float32),
            pltpu.VMEM((tiles, rows, HD), jnp.bfloat16),
            pltpu.VMEM((tiles, count * token_count, HD), jnp.bfloat16),
        ],
        compiler_params=pltpu.CompilerParams(vmem_limit_bytes=10 << 20),
        cost_estimate=pl.CostEstimate(
            flops=count * tiles * 4 * token_count * key_count * HD,
            transcendentals=count * tiles * token_count * key_count,
            bytes_accessed=3 * own.size * 2,
        ),
        name="attend",
    )(me, ids, *in_vmem(*qr, q_features, own, first, second, k_features))


def grid_lanes(tile_rows, tile_cols):
    token_count = tile_rows * tile_cols
    lane = lax.broadcasted_iota(jnp.int32, (token_count, HD), 1)
    token = lax.broadcasted_iota(jnp.int32, (token_count, HD), 0)
    row, col = lax.div(token, tile_cols), lax.rem(token, tile_cols)
    is_row = lane < tile_rows
    is_col = (lane >= tile_rows) & (lane < tile_rows + tile_cols)
    is_flag = lane == tile_rows + tile_cols
    return lane, row, col, is_row, is_col, is_flag


def query_features_kernel(tile_rows, tile_cols, me_ref, *refs):
    *come, o_ref = refs
    lane, row, col, is_row, is_col, is_flag = grid_lanes(tile_rows, tile_cols)
    hot = ((is_row & (lane == row)) | (is_col & (lane - tile_rows == col))).astype(jnp.float32)
    token = row * tile_cols + col
    for k, ref in enumerate(come):
        flags = ref[...].astype(jnp.float32)
        flag = jnp.zeros(hot.shape, jnp.float32)
        for part in range(tile_rows * tile_cols // HD):
            flag += jnp.where(token - part * HD == lane, flags[part : part + 1], 0.0)
        column = jnp.sum(flag, axis=1, keepdims=True)
        o_ref[me_ref[0] ^ k] = jnp.where(is_flag, 1.0 - column, hot).astype(jnp.bfloat16)


def query_features(tile_rows, tile_cols, me, come):
    tiles = len(come)
    last = come[0].shape[0] // 16 - 1
    return pl.pallas_call(
        functools.partial(query_features_kernel, tile_rows, tile_cols),
        grid=(1,),
        out_shape=jax.ShapeDtypeStruct((tiles, tile_rows * tile_cols, HD), jnp.bfloat16),
        in_specs=[SMEM] + [pl.BlockSpec((16, HD), lambda i: (last, 0))] * tiles,
        out_specs=VMEM,
        compiler_params=pltpu.CompilerParams(vmem_limit_bytes=4 << 20),
        name="query_features",
    )(me, *come)


def key_features_kernel(tile_rows, tile_cols, side_ref, o_ref):
    lane, row, col, is_row, is_col, is_flag = grid_lanes(tile_rows, tile_cols)
    far_rows = []
    for slot in range(2):
        toward, there = side_ref[slot, 0], side_ref[slot, 1]
        beyond = (row - lane) * toward > 0
        far_rows.append(jnp.where(is_row & (beyond | (there == 0)), FAR, 0.0))
    near = jnp.zeros_like(far_rows[0])
    far_rows = [far_rows[0], near, far_rows[1]]
    far_cols = [
        jnp.where(is_col & (col < lane - tile_rows), FAR, 0.0),
        near,
        jnp.where(is_col & (col > lane - tile_rows), FAR, 0.0),
    ]
    for r in range(3):
        for c in range(3):
            o_ref[r, c] = (far_rows[r] + far_cols[c]).astype(jnp.bfloat16)
    for c in range(3):
        o_ref[3, c] = jnp.where(is_flag, FAR, 0.0).astype(jnp.bfloat16)


def key_features(tile_rows, tile_cols, sides):
    return pl.pallas_call(
        functools.partial(key_features_kernel, tile_rows, tile_cols),
        out_shape=jax.ShapeDtypeStruct((4, 3, tile_rows * tile_cols, HD), jnp.bfloat16),
        in_specs=[SMEM],
        out_specs=VMEM,
        compiler_params=pltpu.CompilerParams(vmem_limit_bytes=4 << 20),
        name="key_features",
    )(sides)


def pack_kv_kernel(tiles, share, heads, me_ref, x_ref, *refs):
    *o_refs, sem = refs
    pairs = []
    for k, o_ref in enumerate(o_refs):
        for n, head in enumerate(heads):
            first = pl.multiple_of(((me_ref[0] ^ k) * share + head) * HD, HD)
            pairs.append((x_ref.at[:, :, pl.ds(first, HD)], o_ref.at[2 * n : 2 * n + 2]))
    copied(pairs, sem)


def pack_kv(me, x, heads, tiles, share):
    shape = jax.ShapeDtypeStruct((2 * len(heads), x.shape[1], HD), x.dtype)
    return pl.pallas_call(
        functools.partial(pack_kv_kernel, tiles, share, heads),
        out_shape=[shape] * tiles,
        in_specs=[SMEM, ANY],
        out_specs=[VMEM] * tiles,
        scratch_shapes=[pltpu.SemaphoreType.DMA((tiles * len(heads),))],
        compiler_params=pltpu.CompilerParams(vmem_limit_bytes=8 << 20),
        name="pack_kv",
    )(me, x)


def order_kernel(me_ref, *refs):
    *come, o_ref, sem = refs
    copied([(ref, o_ref.at[me_ref[0] ^ k]) for k, ref in enumerate(come)], sem)


def order(me, come):
    tiles = len(come)
    return pl.pallas_call(
        order_kernel,
        out_shape=jax.ShapeDtypeStruct((tiles, *come[0].shape), come[0].dtype),
        in_specs=[SMEM] + [ANY] * tiles,
        out_specs=VMEM,
        scratch_shapes=[pltpu.SemaphoreType.DMA((tiles,))],
        compiler_params=pltpu.CompilerParams(vmem_limit_bytes=6 << 20),
        name="order",
    )(me, *come)


def pack_qr_kernel(tiles, share, chunks, me_ref, q_ref, r_ref, f_ref, *refs):
    *o_refs, sem = refs
    token_count = q_ref.shape[0]
    block_tokens = r_ref.shape[1]
    pairs = []
    for c, heads in enumerate(chunks):
        for k in range(tiles):
            o_ref = o_refs[c * tiles + k]
            at = 0
            for head in heads:
                lanes = pl.ds(pl.multiple_of(((me_ref[0] ^ k) * share + head) * HD, HD), HD)
                pairs.append((q_ref.at[:, lanes], o_ref.at[at : at + token_count]))
                at += token_count
                for part in range(2):
                    pairs.append((r_ref.at[part, :, lanes], o_ref.at[at : at + block_tokens]))
                    at += block_tokens
            if f_ref.shape[0] + at == o_ref.shape[0]:
                pairs.append((f_ref, o_ref.at[at : at + f_ref.shape[0]]))
    copied(pairs, sem)


def pack_qr(me, q, r, f, chunks, tiles, share):
    rows = q.shape[0] + 2 * r.shape[1]
    shapes = [
        jax.ShapeDtypeStruct((rows * len(heads) + (f.shape[0] if heads[0] == 0 else 0), HD), q.dtype)
        for c, heads in enumerate(chunks)
        for k in range(tiles)
    ]
    flat = pl.pallas_call(
        functools.partial(pack_qr_kernel, tiles, share, chunks),
        out_shape=shapes,
        in_specs=[SMEM] + [ANY] * 3,
        out_specs=[VMEM] * len(shapes),
        scratch_shapes=[pltpu.SemaphoreType.DMA((tiles * (3 * share + 1),))],
        compiler_params=pltpu.CompilerParams(vmem_limit_bytes=8 << 20),
        name="pack_qr",
    )(me, q, r, f)
    return [flat[n * tiles : (n + 1) * tiles] for n in range(len(chunks))]


def fetch_rows(tiles, share, chunk, me_ref, w_hbm, w_ref, sem, columns):
    depth = len(chunk) * HD
    copies = []
    for k in range(tiles):
        first = pl.multiple_of(((me_ref[0] ^ k) * share + chunk[0]) * HD, HD)
        copies.append(
            pltpu.make_async_copy(
                w_hbm.at[pl.ds(first, depth), columns], w_ref.at[k], sem.at[k]
            )
        )
        copies[-1].start()
    return copies


def side_by_side(ref, count):
    token_count = ref.shape[0] // count
    return jnp.concatenate(
        [ref[n * token_count : (n + 1) * token_count] for n in range(count)], axis=1
    )


def project_early_kernel(tiles, share, chunk, me_ref, w_hbm, *refs):
    *heads, o_ref, w_ref, sem = refs
    width = o_ref.shape[2]
    copies = fetch_rows(tiles, share, chunk, me_ref, w_hbm, w_ref, sem, slice(None))
    for k in range(tiles):
        copies[k].wait()
        x = side_by_side(heads[k], len(chunk))
        for half in range(2):
            part = jnp.dot(
                x, w_ref[k, :, half * width : (half + 1) * width], preferred_element_type=jnp.float32
            )
            o_ref[half] = part if k == 0 else o_ref[half] + part


def project_early(me, weight, heads, chunk, share):
    tiles = len(heads)
    token_count = heads[0].shape[0] // len(chunk)
    width = weight.shape[1]
    return pl.pallas_call(
        functools.partial(project_early_kernel, tiles, share, chunk),
        out_shape=jax.ShapeDtypeStruct((2, token_count, width // 2), jnp.float32),
        in_specs=[SMEM, ANY] + [VMEM] * tiles,
        out_specs=VMEM,
        scratch_shapes=[
            pltpu.VMEM((tiles, len(chunk) * HD, width), jnp.bfloat16),
            pltpu.SemaphoreType.DMA((tiles,)),
        ],
        compiler_params=pltpu.CompilerParams(vmem_limit_bytes=14 << 20),
        name="project_early",
    )(me, pltpu.with_memory_space_constraint(weight, pltpu.HBM), *heads)


def project_kernel(tiles, share, chunk, me_ref, which_ref, w_hbm, early_ref, *refs):
    *heads, o_ref, w_ref, sem = refs
    width = o_ref.shape[1]
    columns = pl.ds(pl.multiple_of(which_ref[0] * width, HD), width)
    copies = fetch_rows(tiles, share, chunk, me_ref, w_hbm, w_ref, sem, columns)
    total = early_ref[which_ref[0]]
    for copy in copies:
        copy.wait()
    for k in range(tiles):
        x = side_by_side(heads[k], len(chunk))
        total = total + jnp.dot(x, w_ref[k], preferred_element_type=jnp.float32)
    o_ref[...] = total.astype(o_ref.dtype)


def project(me, which, weight, early, heads, chunk, share):
    tiles = len(heads)
    _, token_count, width = early.shape
    return pl.pallas_call(
        functools.partial(project_kernel, tiles, share, chunk),
        out_shape=jax.ShapeDtypeStruct((token_count, width), jnp.bfloat16),
        in_specs=[SMEM] * 2 + [ANY] + [VMEM] * (1 + tiles),
        out_specs=VMEM,
        scratch_shapes=[
            pltpu.VMEM((tiles, len(chunk) * HD, width), jnp.bfloat16),
            pltpu.SemaphoreType.DMA((tiles,)),
        ],
        compiler_params=pltpu.CompilerParams(vmem_limit_bytes=10 << 20),
        name="project",
    )(me, which.reshape(1), pltpu.with_memory_space_constraint(weight, pltpu.HBM), early, *heads)


def in_vmem(*arrays):
    return [pltpu.with_memory_space_constraint(x, pltpu.VMEM) for x in arrays]


def after(x, *others):
    return lax.optimization_barrier((x, *others))[0]


def by_head(queries, keys_values, ref_cache, ref_ids, flags, proj_weight):
    tile_rows, tile_cols, channels = queries.shape
    tiles = lax.axis_size("wa")
    token_count = tile_rows * tile_cols
    share = channels // HD // tiles
    chunks = [list(range(share - 1)), [share - 1]]
    per_owner = ref_cache.shape[0]
    heights = lax.axis_size("ha")
    kv = keys_values.reshape(token_count, 2, channels).transpose(1, 0, 2)

    def swap(come):
        return [
            x if k == 0 else lax.ppermute(x, "wa", [(i, i ^ k) for i in range(tiles)])
            for k, x in enumerate(come)
        ]

    even = [(i, i + 1) for i in range(0, heights - 1, 2)]
    odd = [(i, i + 1) for i in range(1, heights - 1, 2)]
    both_ways = [[(b, a) for a, b in pairs] + pairs for pairs in (even, odd)]

    def neighbours(x):
        return [lax.ppermute(x, "ha", pairs) for pairs in both_ways]

    place = lax.axis_index("ha")
    toward = 1 - 2 * (place % 2)
    sides = jnp.stack(
        [
            jnp.stack([way, ((place + way >= 0) & (place + way < heights)).astype(jnp.int32)])
            for way in (toward, -toward)
        ]
    )
    me = lax.axis_index("wa").reshape(1)
    packed = [pack_kv(me, kv, chunks[0], tiles, share)]
    for chunk in chunks[1:]:
        packed.append(pack_kv(me, after(kv, *packed[-1]), chunk, tiles, share))
    come = [swap(packed[0])]
    for pieces in packed[1:]:
        come.append(swap([after(x, *come[-1][1:]) for x in pieces]))
    own = [order(me, lax.optimization_barrier((*come[0], *packed[-1]))[:tiles])]
    around = [neighbours(own[0])]
    late_q, late_r = lax.optimization_barrier((queries, ref_cache, packed[-1][1]))[:2]
    late_r = late_r.reshape(-1, 2, channels).transpose(1, 0, 2)
    flag_rows = jnp.pad(flags.reshape(-1, HD), ((0, 16 - token_count // HD), (0, 0)))
    late_q = late_q.reshape(token_count, channels)
    flag_rows = flag_rows.astype(jnp.bfloat16)
    qr = pack_qr(me, late_q, late_r, flag_rows, chunks[:1], tiles, share)
    later = lax.optimization_barrier((late_q, late_r, flag_rows, come[-1][1]))[:3]
    qr += pack_qr(me, *later, chunks[1:], tiles, share)
    k_features = key_features(tile_rows, tile_cols, sides)
    for pieces in come[1:]:
        own.append(order(me, lax.optimization_barrier((*pieces, qr[0][1], k_features))[:tiles]))
        around.append(neighbours(after(own[-1], *around[-1])))
    arrived = []
    for n, pieces in enumerate(qr):
        gates = come[-1][1:] if n == 0 else arrived[-1][1:]
        arrived.append(swap([after(x, *gates) for x in pieces]))
    q_features = query_features(tile_rows, tile_cols, me, arrived[0])
    heads = [
        swap(
            attend(
                per_owner, me, ref_ids[0], arrived[n], q_features, own[n], *around[n], k_features
            )
        )
        for n in range(len(chunks))
    ]
    early = project_early(me, proj_weight, heads[0], chunks[0], share)
    mine = lax.axis_index("head")
    theirs = project(me, 1 - mine, proj_weight, early, heads[1], chunks[1], share)
    got = lax.ppermute(theirs, "head", [(0, 1), (1, 0)])
    own_part = project(me, mine, proj_weight, early, heads[1], chunks[1], share)
    total = own_part.astype(jnp.float32) + got.astype(jnp.float32)
    return total.astype(jnp.bfloat16).reshape(tile_rows, tile_cols, -1)


def on_device(queries, *others):
    head_count = queries.shape[2] // HD
    fits = (
        head_count % lax.axis_size("wa") == 0
        and lax.axis_size("wa") & (lax.axis_size("wa") - 1) == 0
        and head_count // lax.axis_size("wa") > 1
        and lax.axis_size("head") == 2
        and queries.shape[0] == RADIUS
        and queries.shape[1] == RADIUS
    )
    return (by_head if fits else by_tile)(queries, *others)


def solution(mesh):
    return jax.shard_map(
        on_device,
        mesh=mesh,
        in_specs=(
            P("ha", "wa", "head"),
            P("ha", "wa", None, "head"),
            P("wa", None, None, "head"),
            P("ha", None, None),
            P("ha", "wa"),
            P("head", None),
        ),
        out_specs=P("ha", "wa", "head"),
        check_vma=False,
    )
```

```python
import functools
import math

import jax
import jax.numpy as jnp
from jax import lax
from jax.experimental import pallas as pl
from jax.experimental.pallas import tpu as pltpu
from jax.sharding import PartitionSpec as P

HD = 128
RADIUS = 16
FAR = -131072.0


def extended(cells, sides, width):
    for axis, dim in sides:
        count = lax.axis_size(axis)
        ends = count - 1
        head = lax.slice_in_dim(cells, 0, width, axis=dim)
        tail = lax.slice_in_dim(cells, cells.shape[dim] - width, cells.shape[dim], axis=dim)
        cells = jnp.concatenate(
            [
                lax.ppermute(tail, axis, [(i, (i + 1) % count) for i in range(ends)]),
                cells,
                lax.ppermute(head, axis, [((i + 1) % count, i) for i in range(ends)]),
            ],
            axis=dim,
        )
    return cells


def by_tile(queries, keys_values, ref_cache, ref_ids, flags, proj_weight):
    tile_rows, tile_cols, channels = queries.shape
    head_count = channels // HD
    padded_rows = tile_rows + 2 * RADIUS
    padded_cols = tile_cols + 2 * RADIUS
    token_count = tile_rows * tile_cols
    score_scale = HD ** (-0.5)
    padded = extended(keys_values, (("ha", 0), ("wa", 1)), RADIUS)
    row_place = lax.axis_index("ha") * tile_rows - RADIUS + jnp.arange(padded_rows, dtype=jnp.int32)
    col_place = lax.axis_index("wa") * tile_cols - RADIUS + jnp.arange(padded_cols, dtype=jnp.int32)
    row_inside = (row_place >= 0) & (row_place < tile_rows * lax.axis_size("ha"))
    col_inside = (col_place >= 0) & (col_place < tile_cols * lax.axis_size("wa"))
    inside = row_inside[:, None] & col_inside[None, :]
    query_row = jnp.arange(tile_rows)[:, None, None, None]
    query_col = jnp.arange(tile_cols)[None, :, None, None]
    key_row = jnp.arange(padded_rows)[None, None, :, None]
    key_col = jnp.arange(padded_cols)[None, None, None, :]
    window = (jnp.abs(key_row - RADIUS - query_row) <= RADIUS) & (
        jnp.abs(key_col - RADIUS - query_col) <= RADIUS
    )
    window = (window & inside[None, None]).reshape(token_count, padded_rows * padded_cols)
    key_flat = padded[:, :, 0].reshape(padded_rows * padded_cols, channels)
    value_flat = padded[:, :, 1].reshape(padded_rows * padded_cols, channels)
    query_flat = queries.reshape(token_count, channels)
    flagged = flags.reshape(token_count) == 1
    wanted = ref_ids[0]
    my_blocks = lax.dynamic_index_in_dim(wanted, lax.axis_index("wa"), 0, keepdims=False)
    per_owner = ref_cache.shape[0]
    target = lax.axis_index("wa") * per_owner + jnp.arange(per_owner, dtype=jnp.int32)
    request_count = jnp.sum((wanted[:, :, None] == target[None, None, :]).astype(jnp.int32), axis=1)
    outgoing = jnp.einsum(
        "wr,rtkc->wtkc",
        request_count.astype(jnp.bfloat16),
        ref_cache,
        preferred_element_type=jnp.float32,
    ).astype(jnp.bfloat16)
    arrived = lax.all_to_all(outgoing, "wa", split_axis=0, concat_axis=0, tiled=True)
    picked = jnp.take(arrived, my_blocks // per_owner, axis=0)
    ref_keys = picked[:, :, 0].reshape(-1, channels)
    ref_values = picked[:, :, 1].reshape(-1, channels)
    head_outputs = []
    for head_index in range(head_count):
        first = head_index * HD
        head_query = query_flat[:, first : first + HD]
        scores = (
            jnp.einsum(
                "qc,kc->qk",
                head_query,
                key_flat[:, first : first + HD],
                preferred_element_type=jnp.float32,
            )
            * score_scale
        )
        scores = jnp.where(window, scores, -jnp.inf)
        row_max = jnp.max(scores, axis=1)
        ref_scores = (
            jnp.einsum(
                "qc,kc->qk",
                head_query,
                ref_keys[:, first : first + HD],
                preferred_element_type=jnp.float32,
            )
            * score_scale
        )
        ref_scores = jnp.where(flagged[:, None], ref_scores, -jnp.inf)
        row_max = jnp.maximum(row_max, jnp.max(ref_scores, axis=1))
        ref_probs = jnp.exp(ref_scores - row_max[:, None])
        ref_total = jnp.sum(ref_probs, axis=1)
        ref_part = jnp.dot(
            ref_probs.astype(jnp.bfloat16),
            ref_values[:, first : first + HD],
            preferred_element_type=jnp.float32,
        )
        probs = jnp.exp(scores - row_max[:, None])
        denominator = jnp.sum(probs, axis=1) + ref_total
        numerator = (
            jnp.dot(
                probs.astype(jnp.bfloat16),
                value_flat[:, first : first + HD],
                preferred_element_type=jnp.float32,
            )
            + ref_part
        )
        head_outputs.append(numerator / denominator[:, None])
    attended = jnp.concatenate(head_outputs, axis=1).astype(jnp.bfloat16)
    partial_term = jnp.dot(attended, proj_weight, preferred_element_type=jnp.float32).reshape(
        tile_rows, tile_cols, -1
    )
    return lax.psum_scatter(
        partial_term.astype(jnp.bfloat16), "head", scatter_dimension=2, tiled=True
    )


VMEM = pl.BlockSpec(memory_space=pltpu.VMEM)
SMEM = pl.BlockSpec(memory_space=pltpu.SMEM)
ANY = pl.BlockSpec(memory_space=pl.ANY)


def copied(pairs, sem):
    copies = [
        pltpu.make_async_copy(source, target, sem.at[n]) for n, (source, target) in enumerate(pairs)
    ]
    for copy in copies:
        copy.start()
    for copy in copies:
        copy.wait()


def attend_kernel(per_owner, tiles, count, me_ref, ids_ref, *refs):
    come, (qf_ref, own_ref, a_ref, b_ref, kf_ref) = refs[:tiles], refs[tiles : tiles + 5]
    o_refs, scratch = refs[tiles + 5 : 2 * tiles + 5], refs[2 * tiles + 5 :]
    s_ref, qr_ref, out_ref = scratch
    token_count = qf_ref.shape[1]
    head_rows = qr_ref.shape[1] // count
    block_tokens = (head_rows - token_count) // 2 // per_owner
    chosen_count = ids_ref.shape[1]
    factor = HD ** (-0.5) * math.log2(math.e)
    ones = jnp.ones((token_count, HD), jnp.bfloat16)
    ones_block = jnp.ones((block_tokens, HD), jnp.bfloat16)
    for k in range(tiles):
        qr_ref[me_ref[0] ^ k] = come[k][: qr_ref.shape[1]]

    def pieces(head, w):
        key_at = head * head_rows + token_count
        value_at = key_at + per_owner * block_tokens
        for other in range(max(w - 1, 0), min(w + 2, tiles)):
            for r, source in enumerate((a_ref, own_ref, b_ref)):
                yield (
                    functools.partial(lambda s, o: s[o, 2 * head], source, other),
                    functools.partial(lambda r, c: kf_ref[r, c], r, other - w + 1),
                    functools.partial(lambda s, o: s[o, 2 * head + 1], source, other),
                )
        for n in range(chosen_count):
            chosen = ids_ref[w, n]
            owner = lax.div(chosen, per_owner)
            start = pl.multiple_of(lax.rem(chosen, per_owner) * block_tokens, block_tokens)
            yield (
                functools.partial(lambda o, s: qr_ref[o, pl.ds(key_at + s, block_tokens)], owner, start),
                lambda: kf_ref[3, 0, :block_tokens],
                functools.partial(lambda o, s: qr_ref[o, pl.ds(value_at + s, block_tokens)], owner, start),
            )

    def score(head, w, slot):
        query_at = head * head_rows
        q_wide = jnp.concatenate(
            [qr_ref[w, query_at : query_at + token_count], qf_ref[w]], axis=1
        )
        at, best = 0, None
        for keys, features, _ in pieces(head, w):
            wide = jnp.concatenate([keys(), features()], axis=1)
            s = lax.dot_general(
                q_wide, wide, (((1,), (1,)), ((), ())), preferred_element_type=jnp.float32
            )
            s_ref[slot, :, at : at + s.shape[1]] = s
            at += s.shape[1]
            for part in range(0, s.shape[1], HD):
                piece = s[:, part : part + HD]
                best = piece if best is None else jnp.maximum(best, piece)
            yield None
        yield jnp.max(best, axis=1, keepdims=True)

    def weigh(head, w, slot, row_max):
        at = 0
        total = jnp.zeros((token_count, 2 * HD), jnp.float32)
        for _, _, values in pieces(head, w):
            v = values()
            width = v.shape[0]
            probs = jnp.exp2((s_ref[slot, :, at : at + width] - row_max) * factor)
            total = total + jnp.dot(
                probs.astype(jnp.bfloat16),
                jnp.concatenate([v, jnp.ones((width, HD), jnp.bfloat16)], axis=1),
                preferred_element_type=jnp.float32,
            )
            at += width
            yield None
        out_ref[w, head * token_count : (head + 1) * token_count] = (
            total[:, :HD] / total[:, HD:]
        ).astype(jnp.bfloat16)

    items = [(head, w) for head in range(count) for w in range(tiles)]
    row_max = None
    for n in range(len(items) + 1):
        first = score(*items[n], n % 2) if n < len(items) else iter(())
        second = weigh(*items[n - 1], 1 - n % 2, row_max) if n else iter(())
        running = [first, second]
        while running:
            for one in list(running):
                try:
                    got = next(one)
                    if got is not None:
                        row_max = got
                except StopIteration:
                    running.remove(one)
    for k in range(tiles):
        o_refs[k][...] = out_ref[me_ref[0] ^ k]


def attend(per_owner, me, ids, qr, q_features, own, first, second, k_features):
    tiles, token_count, _ = q_features.shape
    count = own.shape[1] // 2
    key_count = (9 + ids.shape[1]) * token_count
    rows = qr[0].shape[0] // 128 * 128
    return pl.pallas_call(
        functools.partial(attend_kernel, per_owner, tiles, count),
        out_shape=[jax.ShapeDtypeStruct((count * token_count, HD), jnp.bfloat16)] * tiles,
        in_specs=[SMEM] * 2 + [VMEM] * (tiles + 5),
        out_specs=[VMEM] * tiles,
        scratch_shapes=[
            pltpu.VMEM((2, token_count, key_count), jnp.float32),
            pltpu.VMEM((tiles, rows, HD), jnp.bfloat16),
            pltpu.VMEM((tiles, count * token_count, HD), jnp.bfloat16),
        ],
        compiler_params=pltpu.CompilerParams(vmem_limit_bytes=12 << 20),
        cost_estimate=pl.CostEstimate(
            flops=count * tiles * 4 * token_count * key_count * HD,
            transcendentals=count * tiles * token_count * key_count,
            bytes_accessed=3 * own.size * 2,
        ),
        name="attend",
    )(me, ids, *in_vmem(*qr, q_features, own, first, second, k_features))


def grid_lanes(tile_rows, tile_cols):
    token_count = tile_rows * tile_cols
    lane = lax.broadcasted_iota(jnp.int32, (token_count, HD), 1)
    token = lax.broadcasted_iota(jnp.int32, (token_count, HD), 0)
    row, col = lax.div(token, tile_cols), lax.rem(token, tile_cols)
    is_row = lane < tile_rows
    is_col = (lane >= tile_rows) & (lane < tile_rows + tile_cols)
    is_flag = lane == tile_rows + tile_cols
    return lane, row, col, is_row, is_col, is_flag


def query_features_kernel(tile_rows, tile_cols, me_ref, *refs):
    *come, o_ref = refs
    lane, row, col, is_row, is_col, is_flag = grid_lanes(tile_rows, tile_cols)
    hot = ((is_row & (lane == row)) | (is_col & (lane - tile_rows == col))).astype(jnp.float32)
    token = row * tile_cols + col
    for k, ref in enumerate(come):
        flags = ref[...].astype(jnp.float32)
        flag = jnp.zeros(hot.shape, jnp.float32)
        for part in range(tile_rows * tile_cols // HD):
            flag += jnp.where(token - part * HD == lane, flags[part : part + 1], 0.0)
        column = jnp.sum(flag, axis=1, keepdims=True)
        o_ref[me_ref[0] ^ k] = jnp.where(is_flag, 1.0 - column, hot).astype(jnp.bfloat16)


def query_features(tile_rows, tile_cols, me, come):
    tiles = len(come)
    last = come[0].shape[0] // 16 - 1
    return pl.pallas_call(
        functools.partial(query_features_kernel, tile_rows, tile_cols),
        grid=(1,),
        out_shape=jax.ShapeDtypeStruct((tiles, tile_rows * tile_cols, HD), jnp.bfloat16),
        in_specs=[SMEM] + [pl.BlockSpec((16, HD), lambda i: (last, 0))] * tiles,
        out_specs=VMEM,
        compiler_params=pltpu.CompilerParams(vmem_limit_bytes=4 << 20),
        name="query_features",
    )(me, *come)


def key_features_kernel(tile_rows, tile_cols, side_ref, o_ref):
    lane, row, col, is_row, is_col, is_flag = grid_lanes(tile_rows, tile_cols)
    far_rows = []
    for slot in range(2):
        toward, there = side_ref[slot, 0], side_ref[slot, 1]
        beyond = (row - lane) * toward > 0
        far_rows.append(jnp.where(is_row & (beyond | (there == 0)), FAR, 0.0))
    near = jnp.zeros_like(far_rows[0])
    far_rows = [far_rows[0], near, far_rows[1]]
    far_cols = [
        jnp.where(is_col & (col < lane - tile_rows), FAR, 0.0),
        near,
        jnp.where(is_col & (col > lane - tile_rows), FAR, 0.0),
    ]
    for r in range(3):
        for c in range(3):
            o_ref[r, c] = (far_rows[r] + far_cols[c]).astype(jnp.bfloat16)
    for c in range(3):
        o_ref[3, c] = jnp.where(is_flag, FAR, 0.0).astype(jnp.bfloat16)


def key_features(tile_rows, tile_cols, sides):
    return pl.pallas_call(
        functools.partial(key_features_kernel, tile_rows, tile_cols),
        out_shape=jax.ShapeDtypeStruct((4, 3, tile_rows * tile_cols, HD), jnp.bfloat16),
        in_specs=[SMEM],
        out_specs=VMEM,
        compiler_params=pltpu.CompilerParams(vmem_limit_bytes=4 << 20),
        name="key_features",
    )(sides)


def pack_kv_kernel(tiles, share, heads, me_ref, x_ref, *refs):
    *o_refs, sem = refs
    pairs = []
    for k, o_ref in enumerate(o_refs):
        for n, head in enumerate(heads):
            first = pl.multiple_of(((me_ref[0] ^ k) * share + head) * HD, HD)
            pairs.append((x_ref.at[:, :, pl.ds(first, HD)], o_ref.at[2 * n : 2 * n + 2]))
    copied(pairs, sem)


def pack_kv(me, x, heads, tiles, share):
    shape = jax.ShapeDtypeStruct((2 * len(heads), x.shape[1], HD), x.dtype)
    return pl.pallas_call(
        functools.partial(pack_kv_kernel, tiles, share, heads),
        out_shape=[shape] * tiles,
        in_specs=[SMEM, ANY],
        out_specs=[VMEM] * tiles,
        scratch_shapes=[pltpu.SemaphoreType.DMA((tiles * len(heads),))],
        compiler_params=pltpu.CompilerParams(vmem_limit_bytes=8 << 20),
        name="pack_kv",
    )(me, x)


def order_kernel(me_ref, *refs):
    *come, o_ref, sem = refs
    copied([(ref, o_ref.at[me_ref[0] ^ k]) for k, ref in enumerate(come)], sem)


def order(me, come):
    tiles = len(come)
    return pl.pallas_call(
        order_kernel,
        out_shape=jax.ShapeDtypeStruct((tiles, *come[0].shape), come[0].dtype),
        in_specs=[SMEM] + [ANY] * tiles,
        out_specs=VMEM,
        scratch_shapes=[pltpu.SemaphoreType.DMA((tiles,))],
        compiler_params=pltpu.CompilerParams(vmem_limit_bytes=6 << 20),
        name="order",
    )(me, *come)


def pack_qr_kernel(tiles, share, chunks, me_ref, q_ref, r_ref, f_ref, *refs):
    *o_refs, sem = refs
    token_count = q_ref.shape[0]
    block_tokens = r_ref.shape[1]
    pairs = []
    for c, heads in enumerate(chunks):
        for k in range(tiles):
            o_ref = o_refs[c * tiles + k]
            at = 0
            for head in heads:
                lanes = pl.ds(pl.multiple_of(((me_ref[0] ^ k) * share + head) * HD, HD), HD)
                pairs.append((q_ref.at[:, lanes], o_ref.at[at : at + token_count]))
                at += token_count
                for part in range(2):
                    pairs.append((r_ref.at[part, :, lanes], o_ref.at[at : at + block_tokens]))
                    at += block_tokens
            if f_ref.shape[0] + at == o_ref.shape[0]:
                pairs.append((f_ref, o_ref.at[at : at + f_ref.shape[0]]))
    copied(pairs, sem)


def pack_qr(me, q, r, f, chunks, tiles, share):
    rows = q.shape[0] + 2 * r.shape[1]
    shapes = [
        jax.ShapeDtypeStruct((rows * len(heads) + (f.shape[0] if heads[0] == 0 else 0), HD), q.dtype)
        for c, heads in enumerate(chunks)
        for k in range(tiles)
    ]
    flat = pl.pallas_call(
        functools.partial(pack_qr_kernel, tiles, share, chunks),
        out_shape=shapes,
        in_specs=[SMEM] + [ANY] * 3,
        out_specs=[VMEM] * len(shapes),
        scratch_shapes=[pltpu.SemaphoreType.DMA((tiles * (3 * share + 1),))],
        compiler_params=pltpu.CompilerParams(vmem_limit_bytes=8 << 20),
        name="pack_qr",
    )(me, q, r, f)
    return [flat[n * tiles : (n + 1) * tiles] for n in range(len(chunks))]


def fetch_rows(tiles, share, chunk, me_ref, w_hbm, w_ref, sem):
    depth = len(chunk) * HD
    copies = []
    for k in range(tiles):
        first = pl.multiple_of(((me_ref[0] ^ k) * share + chunk[0]) * HD, HD)
        copies.append(
            pltpu.make_async_copy(
                w_hbm.at[pl.ds(first, depth)], w_ref.at[k], sem.at[k]
            )
        )
        copies[-1].start()
    return copies


def side_by_side(ref, count):
    token_count = ref.shape[0] // count
    return jnp.concatenate(
        [ref[n * token_count : (n + 1) * token_count] for n in range(count)], axis=1
    )


def project_early_kernel(tiles, share, chunks, me_ref, w_hbm, *refs):
    *heads, o_ref, late_ref, w_ref, sem, late_sem = refs
    width = o_ref.shape[2]
    chunk = chunks[0]
    copies = fetch_rows(tiles, share, chunk, me_ref, w_hbm, w_ref, sem)
    late = fetch_rows(tiles, share, chunks[1], me_ref, w_hbm, late_ref, late_sem)
    for k in range(tiles):
        copies[k].wait()
        x = side_by_side(heads[k], len(chunk))
        for half in range(2):
            part = jnp.dot(
                x, w_ref[k, :, half * width : (half + 1) * width], preferred_element_type=jnp.float32
            )
            o_ref[half] = part if k == 0 else o_ref[half] + part
    for copy in late:
        copy.wait()


def project_early(me, weight, heads, chunks, share):
    chunk = chunks[0]
    tiles = len(heads)
    token_count = heads[0].shape[0] // len(chunk)
    width = weight.shape[1]
    return pl.pallas_call(
        functools.partial(project_early_kernel, tiles, share, chunks),
        out_shape=[
            jax.ShapeDtypeStruct((2, token_count, width // 2), jnp.float32),
            jax.ShapeDtypeStruct((tiles, len(chunks[1]) * HD, width), weight.dtype),
        ],
        in_specs=[SMEM, ANY] + [VMEM] * tiles,
        out_specs=[VMEM] * 2,
        scratch_shapes=[
            pltpu.VMEM((tiles, len(chunk) * HD, width), jnp.bfloat16),
            pltpu.SemaphoreType.DMA((tiles,)),
            pltpu.SemaphoreType.DMA((tiles,)),
        ],
        compiler_params=pltpu.CompilerParams(vmem_limit_bytes=18 << 20),
        name="project_early",
    )(me, pltpu.with_memory_space_constraint(weight, pltpu.HBM), *heads)


def project_kernel(tiles, count, which_ref, w_ref, early_ref, *refs):
    *heads, o_ref = refs
    width = o_ref.shape[1]
    columns = pl.ds(pl.multiple_of(which_ref[0] * width, HD), width)
    total = early_ref[which_ref[0]]
    for k in range(tiles):
        total = total + jnp.dot(
            side_by_side(heads[k], count), w_ref[k, :, columns], preferred_element_type=jnp.float32
        )
    o_ref[...] = total.astype(o_ref.dtype)


def project(which, weight, early, heads, count):
    tiles = len(heads)
    _, token_count, width = early.shape
    return pl.pallas_call(
        functools.partial(project_kernel, tiles, count),
        out_shape=jax.ShapeDtypeStruct((token_count, width), jnp.bfloat16),
        in_specs=[SMEM] + [VMEM] * (2 + tiles),
        out_specs=VMEM,
        compiler_params=pltpu.CompilerParams(vmem_limit_bytes=10 << 20),
        name="project",
    )(which.reshape(1), weight, early, *heads)


def in_vmem(*arrays):
    return [pltpu.with_memory_space_constraint(x, pltpu.VMEM) for x in arrays]


def after(x, *others):
    return lax.optimization_barrier((x, *others))[0]


def by_head(queries, keys_values, ref_cache, ref_ids, flags, proj_weight):
    tile_rows, tile_cols, channels = queries.shape
    tiles = lax.axis_size("wa")
    token_count = tile_rows * tile_cols
    share = channels // HD // tiles
    chunks = [list(range(share - 1)), [share - 1]]
    per_owner = ref_cache.shape[0]
    heights = lax.axis_size("ha")
    kv = keys_values.reshape(token_count, 2, channels).transpose(1, 0, 2)

    def swap(come):
        return [
            x if k == 0 else lax.ppermute(x, "wa", [(i, i ^ k) for i in range(tiles)])
            for k, x in enumerate(come)
        ]

    even = [(i, i + 1) for i in range(0, heights - 1, 2)]
    odd = [(i, i + 1) for i in range(1, heights - 1, 2)]
    both_ways = [[(b, a) for a, b in pairs] + pairs for pairs in (even, odd)]

    def neighbours(x):
        return [lax.ppermute(x, "ha", pairs) for pairs in both_ways]

    place = lax.axis_index("ha")
    toward = 1 - 2 * (place % 2)
    sides = jnp.stack(
        [
            jnp.stack([way, ((place + way >= 0) & (place + way < heights)).astype(jnp.int32)])
            for way in (toward, -toward)
        ]
    )
    me = lax.axis_index("wa").reshape(1)
    packed = [pack_kv(me, kv, chunks[0], tiles, share)]
    for chunk in chunks[1:]:
        packed.append(pack_kv(me, after(kv, *packed[-1]), chunk, tiles, share))
    come = [swap(packed[0])]
    for pieces in packed[1:]:
        come.append(swap([after(x, *come[-1][1:]) for x in pieces]))
    own = [order(me, lax.optimization_barrier((*come[0], *packed[-1]))[:tiles])]
    around = [neighbours(own[0])]
    late_q, late_r = lax.optimization_barrier((queries, ref_cache, packed[-1][1]))[:2]
    late_r = late_r.reshape(-1, 2, channels).transpose(1, 0, 2)
    flag_rows = jnp.pad(flags.reshape(-1, HD), ((0, 16 - token_count // HD), (0, 0)))
    late_q = late_q.reshape(token_count, channels)
    flag_rows = flag_rows.astype(jnp.bfloat16)
    qr = pack_qr(me, late_q, late_r, flag_rows, chunks[:1], tiles, share)
    later = lax.optimization_barrier((late_q, late_r, flag_rows, come[-1][1]))[:3]
    qr += pack_qr(me, *later, chunks[1:], tiles, share)
    k_features = key_features(tile_rows, tile_cols, sides)
    for pieces in come[1:]:
        own.append(order(me, lax.optimization_barrier((*pieces, qr[0][1], k_features))[:tiles]))
        around.append(neighbours(after(own[-1], *around[-1])))
    arrived = []
    for n, pieces in enumerate(qr):
        gates = come[-1][1:] if n == 0 else arrived[-1][1:]
        arrived.append(swap([after(x, *gates) for x in pieces]))
    q_features = query_features(tile_rows, tile_cols, me, arrived[0])
    heads = [
        swap(
            attend(
                per_owner, me, ref_ids[0], arrived[n], q_features, own[n], *around[n], k_features
            )
        )
        for n in range(len(chunks))
    ]
    early, weight = project_early(me, proj_weight, heads[0], chunks, share)
    mine = lax.axis_index("head")
    theirs = project(1 - mine, weight, early, heads[1], len(chunks[1]))
    got = lax.ppermute(theirs, "head", [(0, 1), (1, 0)])
    own_part = project(mine, weight, early, heads[1], len(chunks[1]))
    total = own_part.astype(jnp.float32) + got.astype(jnp.float32)
    return total.astype(jnp.bfloat16).reshape(tile_rows, tile_cols, -1)


def on_device(queries, *others):
    head_count = queries.shape[2] // HD
    fits = (
        head_count % lax.axis_size("wa") == 0
        and lax.axis_size("wa") & (lax.axis_size("wa") - 1) == 0
        and head_count // lax.axis_size("wa") > 1
        and lax.axis_size("head") == 2
        and queries.shape[0] == RADIUS
        and queries.shape[1] == RADIUS
    )
    return (by_head if fits else by_tile)(queries, *others)


def solution(mesh):
    return jax.shard_map(
        on_device,
        mesh=mesh,
        in_specs=(
            P("ha", "wa", "head"),
            P("ha", "wa", None, "head"),
            P("wa", None, None, "head"),
            P("ha", None, None),
            P("ha", "wa"),
            P("head", None),
        ),
        out_specs=P("ha", "wa", "head"),
        check_vma=False,
    )
```

```python
import functools
import math

import jax
import jax.numpy as jnp
from jax import lax
from jax.experimental import pallas as pl
from jax.experimental.pallas import tpu as pltpu
from jax.sharding import PartitionSpec as P

HD = 128
RADIUS = 16
FAR = -131072.0


def extended(cells, sides, width):
    for axis, dim in sides:
        count = lax.axis_size(axis)
        ends = count - 1
        head = lax.slice_in_dim(cells, 0, width, axis=dim)
        tail = lax.slice_in_dim(cells, cells.shape[dim] - width, cells.shape[dim], axis=dim)
        cells = jnp.concatenate(
            [
                lax.ppermute(tail, axis, [(i, (i + 1) % count) for i in range(ends)]),
                cells,
                lax.ppermute(head, axis, [((i + 1) % count, i) for i in range(ends)]),
            ],
            axis=dim,
        )
    return cells


def by_tile(queries, keys_values, ref_cache, ref_ids, flags, proj_weight):
    tile_rows, tile_cols, channels = queries.shape
    head_count = channels // HD
    padded_rows = tile_rows + 2 * RADIUS
    padded_cols = tile_cols + 2 * RADIUS
    token_count = tile_rows * tile_cols
    score_scale = HD ** (-0.5)
    padded = extended(keys_values, (("ha", 0), ("wa", 1)), RADIUS)
    row_place = lax.axis_index("ha") * tile_rows - RADIUS + jnp.arange(padded_rows, dtype=jnp.int32)
    col_place = lax.axis_index("wa") * tile_cols - RADIUS + jnp.arange(padded_cols, dtype=jnp.int32)
    row_inside = (row_place >= 0) & (row_place < tile_rows * lax.axis_size("ha"))
    col_inside = (col_place >= 0) & (col_place < tile_cols * lax.axis_size("wa"))
    inside = row_inside[:, None] & col_inside[None, :]
    query_row = jnp.arange(tile_rows)[:, None, None, None]
    query_col = jnp.arange(tile_cols)[None, :, None, None]
    key_row = jnp.arange(padded_rows)[None, None, :, None]
    key_col = jnp.arange(padded_cols)[None, None, None, :]
    window = (jnp.abs(key_row - RADIUS - query_row) <= RADIUS) & (
        jnp.abs(key_col - RADIUS - query_col) <= RADIUS
    )
    window = (window & inside[None, None]).reshape(token_count, padded_rows * padded_cols)
    key_flat = padded[:, :, 0].reshape(padded_rows * padded_cols, channels)
    value_flat = padded[:, :, 1].reshape(padded_rows * padded_cols, channels)
    query_flat = queries.reshape(token_count, channels)
    flagged = flags.reshape(token_count) == 1
    wanted = ref_ids[0]
    my_blocks = lax.dynamic_index_in_dim(wanted, lax.axis_index("wa"), 0, keepdims=False)
    per_owner = ref_cache.shape[0]
    target = lax.axis_index("wa") * per_owner + jnp.arange(per_owner, dtype=jnp.int32)
    request_count = jnp.sum((wanted[:, :, None] == target[None, None, :]).astype(jnp.int32), axis=1)
    outgoing = jnp.einsum(
        "wr,rtkc->wtkc",
        request_count.astype(jnp.bfloat16),
        ref_cache,
        preferred_element_type=jnp.float32,
    ).astype(jnp.bfloat16)
    arrived = lax.all_to_all(outgoing, "wa", split_axis=0, concat_axis=0, tiled=True)
    picked = jnp.take(arrived, my_blocks // per_owner, axis=0)
    ref_keys = picked[:, :, 0].reshape(-1, channels)
    ref_values = picked[:, :, 1].reshape(-1, channels)
    head_outputs = []
    for head_index in range(head_count):
        first = head_index * HD
        head_query = query_flat[:, first : first + HD]
        scores = (
            jnp.einsum(
                "qc,kc->qk",
                head_query,
                key_flat[:, first : first + HD],
                preferred_element_type=jnp.float32,
            )
            * score_scale
        )
        scores = jnp.where(window, scores, -jnp.inf)
        row_max = jnp.max(scores, axis=1)
        ref_scores = (
            jnp.einsum(
                "qc,kc->qk",
                head_query,
                ref_keys[:, first : first + HD],
                preferred_element_type=jnp.float32,
            )
            * score_scale
        )
        ref_scores = jnp.where(flagged[:, None], ref_scores, -jnp.inf)
        row_max = jnp.maximum(row_max, jnp.max(ref_scores, axis=1))
        ref_probs = jnp.exp(ref_scores - row_max[:, None])
        ref_total = jnp.sum(ref_probs, axis=1)
        ref_part = jnp.dot(
            ref_probs.astype(jnp.bfloat16),
            ref_values[:, first : first + HD],
            preferred_element_type=jnp.float32,
        )
        probs = jnp.exp(scores - row_max[:, None])
        denominator = jnp.sum(probs, axis=1) + ref_total
        numerator = (
            jnp.dot(
                probs.astype(jnp.bfloat16),
                value_flat[:, first : first + HD],
                preferred_element_type=jnp.float32,
            )
            + ref_part
        )
        head_outputs.append(numerator / denominator[:, None])
    attended = jnp.concatenate(head_outputs, axis=1).astype(jnp.bfloat16)
    partial_term = jnp.dot(attended, proj_weight, preferred_element_type=jnp.float32).reshape(
        tile_rows, tile_cols, -1
    )
    return lax.psum_scatter(
        partial_term.astype(jnp.bfloat16), "head", scatter_dimension=2, tiled=True
    )


VMEM = pl.BlockSpec(memory_space=pltpu.VMEM)
SMEM = pl.BlockSpec(memory_space=pltpu.SMEM)
ANY = pl.BlockSpec(memory_space=pl.ANY)


def copied(pairs, sem):
    copies = [
        pltpu.make_async_copy(source, target, sem.at[n]) for n, (source, target) in enumerate(pairs)
    ]
    for copy in copies:
        copy.start()
    for copy in copies:
        copy.wait()


def attend_kernel(per_owner, tiles, count, me_ref, ids_ref, *refs):
    come, (qf_ref, own_ref, a_ref, b_ref, kf_ref) = refs[:tiles], refs[tiles : tiles + 5]
    o_refs, scratch = refs[tiles + 5 : 2 * tiles + 5], refs[2 * tiles + 5 :]
    s_ref, qr_ref, out_ref = scratch
    token_count = qf_ref.shape[1]
    head_rows = qr_ref.shape[1] // count
    block_tokens = (head_rows - token_count) // 2 // per_owner
    chosen_count = ids_ref.shape[1]
    factor = HD ** (-0.5) * math.log2(math.e)
    ones = jnp.ones((token_count, HD), jnp.bfloat16)
    ones_block = jnp.ones((block_tokens, HD), jnp.bfloat16)
    for k in range(tiles):
        qr_ref[me_ref[0] ^ k] = come[k][: qr_ref.shape[1]]

    def pieces(head, w):
        key_at = head * head_rows + token_count
        value_at = key_at + per_owner * block_tokens
        for other in range(max(w - 1, 0), min(w + 2, tiles)):
            for r, source in enumerate((a_ref, own_ref, b_ref)):
                yield (
                    functools.partial(lambda s, o: s[o, 2 * head], source, other),
                    functools.partial(lambda r, c: kf_ref[r, c], r, other - w + 1),
                    functools.partial(lambda s, o: s[o, 2 * head + 1], source, other),
                )
        for n in range(chosen_count):
            chosen = ids_ref[w, n]
            owner = lax.div(chosen, per_owner)
            start = pl.multiple_of(lax.rem(chosen, per_owner) * block_tokens, block_tokens)
            yield (
                functools.partial(lambda o, s: qr_ref[o, pl.ds(key_at + s, block_tokens)], owner, start),
                lambda: kf_ref[3, 0, :block_tokens],
                functools.partial(lambda o, s: qr_ref[o, pl.ds(value_at + s, block_tokens)], owner, start),
            )

    def score(head, w, slot):
        query_at = head * head_rows
        q_wide = jnp.concatenate(
            [qr_ref[w, query_at : query_at + token_count], qf_ref[w]], axis=1
        )
        at, best = 0, None
        for keys, features, _ in pieces(head, w):
            wide = jnp.concatenate([keys(), features()], axis=1)
            s = lax.dot_general(
                q_wide, wide, (((1,), (1,)), ((), ())), preferred_element_type=jnp.float32
            )
            s_ref[slot, :, at : at + s.shape[1]] = s
            at += s.shape[1]
            for part in range(0, s.shape[1], HD):
                piece = s[:, part : part + HD]
                best = piece if best is None else jnp.maximum(best, piece)
            yield None
        yield jnp.max(best, axis=1, keepdims=True)

    def weigh(head, w, slot, row_max):
        at = 0
        total = jnp.zeros((token_count, 2 * HD), jnp.float32)
        for _, _, values in pieces(head, w):
            v = values()
            width = v.shape[0]
            probs = jnp.exp2((s_ref[slot, :, at : at + width] - row_max) * factor)
            total = total + jnp.dot(
                probs.astype(jnp.bfloat16),
                jnp.concatenate([v, jnp.ones((width, HD), jnp.bfloat16)], axis=1),
                preferred_element_type=jnp.float32,
            )
            at += width
            yield None
        out_ref[w, head * token_count : (head + 1) * token_count] = (
            total[:, :HD] / total[:, HD:]
        ).astype(jnp.bfloat16)

    items = [(head, w) for head in range(count) for w in range(tiles)]
    row_max = None
    for n in range(len(items) + 1):
        first = score(*items[n], n % 2) if n < len(items) else iter(())
        second = weigh(*items[n - 1], 1 - n % 2, row_max) if n else iter(())
        running = [first, second]
        while running:
            for one in list(running):
                try:
                    got = next(one)
                    if got is not None:
                        row_max = got
                except StopIteration:
                    running.remove(one)
    for k in range(tiles):
        o_refs[k][...] = out_ref[me_ref[0] ^ k]


def attend(per_owner, me, ids, qr, q_features, own, first, second, k_features):
    tiles, token_count, _ = q_features.shape
    count = own.shape[1] // 2
    key_count = (9 + ids.shape[1]) * token_count
    rows = qr[0].shape[0] // 128 * 128
    return pl.pallas_call(
        functools.partial(attend_kernel, per_owner, tiles, count),
        out_shape=[jax.ShapeDtypeStruct((count * token_count, HD), jnp.bfloat16)] * tiles,
        in_specs=[SMEM] * 2 + [VMEM] * (tiles + 5),
        out_specs=[VMEM] * tiles,
        scratch_shapes=[
            pltpu.VMEM((2, token_count, key_count), jnp.float32),
            pltpu.VMEM((tiles, rows, HD), jnp.bfloat16),
            pltpu.VMEM((tiles, count * token_count, HD), jnp.bfloat16),
        ],
        compiler_params=pltpu.CompilerParams(vmem_limit_bytes=12 << 20),
        cost_estimate=pl.CostEstimate(
            flops=count * tiles * 4 * token_count * key_count * HD,
            transcendentals=count * tiles * token_count * key_count,
            bytes_accessed=3 * own.size * 2,
        ),
        name="attend",
    )(me, ids, *in_vmem(*qr, q_features, own, first, second, k_features))


def grid_lanes(tile_rows, tile_cols):
    token_count = tile_rows * tile_cols
    lane = lax.broadcasted_iota(jnp.int32, (token_count, HD), 1)
    token = lax.broadcasted_iota(jnp.int32, (token_count, HD), 0)
    row, col = lax.div(token, tile_cols), lax.rem(token, tile_cols)
    is_row = lane < tile_rows
    is_col = (lane >= tile_rows) & (lane < tile_rows + tile_cols)
    is_flag = lane == tile_rows + tile_cols
    return lane, row, col, is_row, is_col, is_flag


def query_features_kernel(tile_rows, tile_cols, me_ref, *refs):
    *come, o_ref = refs
    lane, row, col, is_row, is_col, is_flag = grid_lanes(tile_rows, tile_cols)
    hot = ((is_row & (lane == row)) | (is_col & (lane - tile_rows == col))).astype(jnp.float32)
    token = row * tile_cols + col
    for k, ref in enumerate(come):
        flags = ref[...].astype(jnp.float32)
        flag = jnp.zeros(hot.shape, jnp.float32)
        for part in range(tile_rows * tile_cols // HD):
            flag += jnp.where(token - part * HD == lane, flags[part : part + 1], 0.0)
        column = jnp.sum(flag, axis=1, keepdims=True)
        o_ref[me_ref[0] ^ k] = jnp.where(is_flag, 1.0 - column, hot).astype(jnp.bfloat16)


def query_features(tile_rows, tile_cols, me, come):
    tiles = len(come)
    last = come[0].shape[0] // 16 - 1
    return pl.pallas_call(
        functools.partial(query_features_kernel, tile_rows, tile_cols),
        grid=(1,),
        out_shape=jax.ShapeDtypeStruct((tiles, tile_rows * tile_cols, HD), jnp.bfloat16),
        in_specs=[SMEM] + [pl.BlockSpec((16, HD), lambda i: (last, 0))] * tiles,
        out_specs=VMEM,
        compiler_params=pltpu.CompilerParams(vmem_limit_bytes=4 << 20),
        name="query_features",
    )(me, *come)


def key_features_kernel(tile_rows, tile_cols, side_ref, o_ref):
    lane, row, col, is_row, is_col, is_flag = grid_lanes(tile_rows, tile_cols)
    far_rows = []
    for slot in range(2):
        toward, there = side_ref[slot, 0], side_ref[slot, 1]
        beyond = (row - lane) * toward > 0
        far_rows.append(jnp.where(is_row & (beyond | (there == 0)), FAR, 0.0))
    near = jnp.zeros_like(far_rows[0])
    far_rows = [far_rows[0], near, far_rows[1]]
    far_cols = [
        jnp.where(is_col & (col < lane - tile_rows), FAR, 0.0),
        near,
        jnp.where(is_col & (col > lane - tile_rows), FAR, 0.0),
    ]
    for r in range(3):
        for c in range(3):
            o_ref[r, c] = (far_rows[r] + far_cols[c]).astype(jnp.bfloat16)
    for c in range(3):
        o_ref[3, c] = jnp.where(is_flag, FAR, 0.0).astype(jnp.bfloat16)


def key_features(tile_rows, tile_cols, sides):
    return pl.pallas_call(
        functools.partial(key_features_kernel, tile_rows, tile_cols),
        out_shape=jax.ShapeDtypeStruct((4, 3, tile_rows * tile_cols, HD), jnp.bfloat16),
        in_specs=[SMEM],
        out_specs=VMEM,
        compiler_params=pltpu.CompilerParams(vmem_limit_bytes=4 << 20),
        name="key_features",
    )(sides)


def pack_kv_kernel(tiles, share, heads, me_ref, x_ref, *refs):
    *o_refs, sem = refs
    pairs = []
    for k, o_ref in enumerate(o_refs):
        for n, head in enumerate(heads):
            first = pl.multiple_of(((me_ref[0] ^ k) * share + head) * HD, HD)
            pairs.append((x_ref.at[:, :, pl.ds(first, HD)], o_ref.at[2 * n : 2 * n + 2]))
    copied(pairs, sem)


def pack_kv(me, x, heads, tiles, share):
    shape = jax.ShapeDtypeStruct((2 * len(heads), x.shape[1], HD), x.dtype)
    return pl.pallas_call(
        functools.partial(pack_kv_kernel, tiles, share, heads),
        out_shape=[shape] * tiles,
        in_specs=[SMEM, ANY],
        out_specs=[VMEM] * tiles,
        scratch_shapes=[pltpu.SemaphoreType.DMA((tiles * len(heads),))],
        compiler_params=pltpu.CompilerParams(vmem_limit_bytes=8 << 20),
        name="pack_kv",
    )(me, x)


def order_kernel(me_ref, *refs):
    *come, o_ref, sem = refs
    copied([(ref, o_ref.at[me_ref[0] ^ k]) for k, ref in enumerate(come)], sem)


def order(me, come):
    tiles = len(come)
    return pl.pallas_call(
        order_kernel,
        out_shape=jax.ShapeDtypeStruct((tiles, *come[0].shape), come[0].dtype),
        in_specs=[SMEM] + [ANY] * tiles,
        out_specs=VMEM,
        scratch_shapes=[pltpu.SemaphoreType.DMA((tiles,))],
        compiler_params=pltpu.CompilerParams(vmem_limit_bytes=6 << 20),
        name="order",
    )(me, *come)


def pack_qr_kernel(tiles, share, chunks, me_ref, q_ref, r_ref, f_ref, *refs):
    *o_refs, sem = refs
    token_count = q_ref.shape[0]
    block_tokens = r_ref.shape[1]
    pairs = []
    for c, heads in enumerate(chunks):
        for k in range(tiles):
            o_ref = o_refs[c * tiles + k]
            at = 0
            for head in heads:
                lanes = pl.ds(pl.multiple_of(((me_ref[0] ^ k) * share + head) * HD, HD), HD)
                pairs.append((q_ref.at[:, lanes], o_ref.at[at : at + token_count]))
                at += token_count
                for part in range(2):
                    pairs.append((r_ref.at[part, :, lanes], o_ref.at[at : at + block_tokens]))
                    at += block_tokens
            if f_ref.shape[0] + at == o_ref.shape[0]:
                pairs.append((f_ref, o_ref.at[at : at + f_ref.shape[0]]))
    copied(pairs, sem)


def pack_qr(me, q, r, f, chunks, tiles, share):
    rows = q.shape[0] + 2 * r.shape[1]
    shapes = [
        jax.ShapeDtypeStruct((rows * len(heads) + (f.shape[0] if heads[0] == 0 else 0), HD), q.dtype)
        for c, heads in enumerate(chunks)
        for k in range(tiles)
    ]
    flat = pl.pallas_call(
        functools.partial(pack_qr_kernel, tiles, share, chunks),
        out_shape=shapes,
        in_specs=[SMEM] + [ANY] * 3,
        out_specs=[VMEM] * len(shapes),
        scratch_shapes=[pltpu.SemaphoreType.DMA((tiles * (3 * share + 1),))],
        compiler_params=pltpu.CompilerParams(vmem_limit_bytes=8 << 20),
        name="pack_qr",
    )(me, q, r, f)
    return [flat[n * tiles : (n + 1) * tiles] for n in range(len(chunks))]


def fetch_rows(tiles, share, chunk, me_ref, w_hbm, w_ref, sem):
    depth = len(chunk) * HD
    copies = []
    for k in range(tiles):
        first = pl.multiple_of(((me_ref[0] ^ k) * share + chunk[0]) * HD, HD)
        copies.append(
            pltpu.make_async_copy(
                w_hbm.at[pl.ds(first, depth)], w_ref.at[k], sem.at[k]
            )
        )
        copies[-1].start()
    return copies


def side_by_side(ref, count):
    token_count = ref.shape[0] // count
    return jnp.concatenate(
        [ref[n * token_count : (n + 1) * token_count] for n in range(count)], axis=1
    )


def project_early_kernel(tiles, share, chunks, me_ref, w_hbm, *refs):
    *heads, o_ref, late_ref, w_ref, sem, late_sem = refs
    width = o_ref.shape[2]
    chunk = chunks[0]
    copies = fetch_rows(tiles, share, chunk, me_ref, w_hbm, w_ref, sem)
    late = fetch_rows(tiles, share, chunks[1], me_ref, w_hbm, late_ref, late_sem)
    for k in range(tiles):
        copies[k].wait()
        x = side_by_side(heads[k], len(chunk))
        for half in range(2):
            part = jnp.dot(
                x, w_ref[k, :, half * width : (half + 1) * width], preferred_element_type=jnp.float32
            )
            o_ref[half] = part if k == 0 else o_ref[half] + part
    for copy in late:
        copy.wait()


def project_early(me, weight, heads, chunks, share):
    chunk = chunks[0]
    tiles = len(heads)
    token_count = heads[0].shape[0] // len(chunk)
    width = weight.shape[1]
    return pl.pallas_call(
        functools.partial(project_early_kernel, tiles, share, chunks),
        out_shape=[
            jax.ShapeDtypeStruct((2, token_count, width // 2), jnp.float32),
            jax.ShapeDtypeStruct((tiles, len(chunks[1]) * HD, width), weight.dtype),
        ],
        in_specs=[SMEM, ANY] + [VMEM] * tiles,
        out_specs=[VMEM] * 2,
        scratch_shapes=[
            pltpu.VMEM((tiles, len(chunk) * HD, width), jnp.bfloat16),
            pltpu.SemaphoreType.DMA((tiles,)),
            pltpu.SemaphoreType.DMA((tiles,)),
        ],
        compiler_params=pltpu.CompilerParams(vmem_limit_bytes=18 << 20),
        name="project_early",
    )(me, pltpu.with_memory_space_constraint(weight, pltpu.HBM), *heads)


def project_kernel(tiles, count, which_ref, w_ref, early_ref, *refs):
    *heads, o_ref = refs
    width = o_ref.shape[1]
    columns = pl.ds(pl.multiple_of(which_ref[0] * width, HD), width)
    total = early_ref[which_ref[0]]
    for k in range(tiles):
        total = total + jnp.dot(
            side_by_side(heads[k], count), w_ref[k, :, columns], preferred_element_type=jnp.float32
        )
    o_ref[...] = total.astype(o_ref.dtype)


def project(which, weight, early, heads, count):
    tiles = len(heads)
    _, token_count, width = early.shape
    return pl.pallas_call(
        functools.partial(project_kernel, tiles, count),
        out_shape=jax.ShapeDtypeStruct((token_count, width), jnp.bfloat16),
        in_specs=[SMEM] + [VMEM] * (2 + tiles),
        out_specs=VMEM,
        compiler_params=pltpu.CompilerParams(vmem_limit_bytes=10 << 20),
        name="project",
    )(which.reshape(1), weight, early, *heads)


def in_vmem(*arrays):
    return [pltpu.with_memory_space_constraint(x, pltpu.VMEM) for x in arrays]


def after(x, *others):
    return lax.optimization_barrier((x, *others))[0]


def by_head(queries, keys_values, ref_cache, ref_ids, flags, proj_weight):
    tile_rows, tile_cols, channels = queries.shape
    tiles = lax.axis_size("wa")
    token_count = tile_rows * tile_cols
    share = channels // HD // tiles
    chunks = [list(range(share - 1)), [share - 1]]
    per_owner = ref_cache.shape[0]
    heights = lax.axis_size("ha")
    kv = keys_values.reshape(token_count, 2, channels).transpose(1, 0, 2)

    def swap(come):
        return [
            x if k == 0 else lax.ppermute(x, "wa", [(i, i ^ k) for i in range(tiles)])
            for k, x in enumerate(come)
        ]

    even = [(i, i + 1) for i in range(0, heights - 1, 2)]
    odd = [(i, i + 1) for i in range(1, heights - 1, 2)]
    both_ways = [[(b, a) for a, b in pairs] + pairs for pairs in (even, odd)]

    def neighbours(x):
        return [lax.ppermute(x, "ha", pairs) for pairs in both_ways]

    place = lax.axis_index("ha")
    toward = 1 - 2 * (place % 2)
    sides = jnp.stack(
        [
            jnp.stack([way, ((place + way >= 0) & (place + way < heights)).astype(jnp.int32)])
            for way in (toward, -toward)
        ]
    )
    me = lax.axis_index("wa").reshape(1)
    packed = [pack_kv(me, kv, chunks[0], tiles, share)]
    for chunk in chunks[1:]:
        packed.append(pack_kv(me, after(kv, *packed[-1]), chunk, tiles, share))
    come = [swap(packed[0])]
    for pieces in packed[1:]:
        come.append(swap([after(x, *come[-1][1:]) for x in pieces]))
    own = [order(me, lax.optimization_barrier((*come[0], *packed[-1]))[:tiles])]
    around = [neighbours(own[0])]
    late_q, late_r = lax.optimization_barrier((queries, ref_cache, packed[-1][1]))[:2]
    late_r = late_r.reshape(-1, 2, channels).transpose(1, 0, 2)
    flag_rows = jnp.pad(flags.reshape(-1, HD), ((0, 16 - token_count // HD), (0, 0)))
    late_q = late_q.reshape(token_count, channels)
    flag_rows = flag_rows.astype(jnp.bfloat16)
    qr = pack_qr(me, late_q, late_r, flag_rows, chunks[:1], tiles, share)
    later = lax.optimization_barrier((late_q, late_r, flag_rows, come[-1][1]))[:3]
    qr += pack_qr(me, *later, chunks[1:], tiles, share)
    k_features = key_features(tile_rows, tile_cols, sides)
    for pieces in come[1:]:
        own.append(order(me, lax.optimization_barrier((*pieces, qr[0][1], k_features))[:tiles]))
        around.append(neighbours(after(own[-1], *around[-1])))
    arrived = []
    for n, pieces in enumerate(qr):
        gates = come[-1] if n == 0 else arrived[-1]
        arrived.append(swap([after(x, gates[max(k, 1)]) for k, x in enumerate(pieces)]))
    q_features = query_features(tile_rows, tile_cols, me, arrived[0])
    heads = [
        swap(
            attend(
                per_owner, me, ref_ids[0], arrived[n], q_features, own[n], *around[n], k_features
            )
        )
        for n in range(len(chunks))
    ]
    early, weight = project_early(me, proj_weight, heads[0], chunks, share)
    mine = lax.axis_index("head")
    theirs = project(1 - mine, weight, early, heads[1], len(chunks[1]))
    got = lax.ppermute(theirs, "head", [(0, 1), (1, 0)])
    own_part = project(mine, weight, early, heads[1], len(chunks[1]))
    total = own_part.astype(jnp.float32) + got.astype(jnp.float32)
    return total.astype(jnp.bfloat16).reshape(tile_rows, tile_cols, -1)


def on_device(queries, *others):
    head_count = queries.shape[2] // HD
    fits = (
        head_count % lax.axis_size("wa") == 0
        and lax.axis_size("wa") & (lax.axis_size("wa") - 1) == 0
        and head_count // lax.axis_size("wa") > 1
        and lax.axis_size("head") == 2
        and queries.shape[0] == RADIUS
        and queries.shape[1] == RADIUS
    )
    return (by_head if fits else by_tile)(queries, *others)


def solution(mesh):
    return jax.shard_map(
        on_device,
        mesh=mesh,
        in_specs=(
            P("ha", "wa", "head"),
            P("ha", "wa", None, "head"),
            P("wa", None, None, "head"),
            P("ha", None, None),
            P("ha", "wa"),
            P("head", None),
        ),
        out_specs=P("ha", "wa", "head"),
        check_vma=False,
    )
```

```python
import functools
import math

import jax
import jax.numpy as jnp
from jax import lax
from jax.experimental import pallas as pl
from jax.experimental.pallas import tpu as pltpu
from jax.sharding import PartitionSpec as P

HD = 128
RADIUS = 16
FAR = -131072.0


def extended(cells, sides, width):
    for axis, dim in sides:
        count = lax.axis_size(axis)
        ends = count - 1
        head = lax.slice_in_dim(cells, 0, width, axis=dim)
        tail = lax.slice_in_dim(cells, cells.shape[dim] - width, cells.shape[dim], axis=dim)
        cells = jnp.concatenate(
            [
                lax.ppermute(tail, axis, [(i, (i + 1) % count) for i in range(ends)]),
                cells,
                lax.ppermute(head, axis, [((i + 1) % count, i) for i in range(ends)]),
            ],
            axis=dim,
        )
    return cells


def by_tile(queries, keys_values, ref_cache, ref_ids, flags, proj_weight):
    tile_rows, tile_cols, channels = queries.shape
    head_count = channels // HD
    padded_rows = tile_rows + 2 * RADIUS
    padded_cols = tile_cols + 2 * RADIUS
    token_count = tile_rows * tile_cols
    score_scale = HD ** (-0.5)
    padded = extended(keys_values, (("ha", 0), ("wa", 1)), RADIUS)
    row_place = lax.axis_index("ha") * tile_rows - RADIUS + jnp.arange(padded_rows, dtype=jnp.int32)
    col_place = lax.axis_index("wa") * tile_cols - RADIUS + jnp.arange(padded_cols, dtype=jnp.int32)
    row_inside = (row_place >= 0) & (row_place < tile_rows * lax.axis_size("ha"))
    col_inside = (col_place >= 0) & (col_place < tile_cols * lax.axis_size("wa"))
    inside = row_inside[:, None] & col_inside[None, :]
    query_row = jnp.arange(tile_rows)[:, None, None, None]
    query_col = jnp.arange(tile_cols)[None, :, None, None]
    key_row = jnp.arange(padded_rows)[None, None, :, None]
    key_col = jnp.arange(padded_cols)[None, None, None, :]
    window = (jnp.abs(key_row - RADIUS - query_row) <= RADIUS) & (
        jnp.abs(key_col - RADIUS - query_col) <= RADIUS
    )
    window = (window & inside[None, None]).reshape(token_count, padded_rows * padded_cols)
    key_flat = padded[:, :, 0].reshape(padded_rows * padded_cols, channels)
    value_flat = padded[:, :, 1].reshape(padded_rows * padded_cols, channels)
    query_flat = queries.reshape(token_count, channels)
    flagged = flags.reshape(token_count) == 1
    wanted = ref_ids[0]
    my_blocks = lax.dynamic_index_in_dim(wanted, lax.axis_index("wa"), 0, keepdims=False)
    per_owner = ref_cache.shape[0]
    target = lax.axis_index("wa") * per_owner + jnp.arange(per_owner, dtype=jnp.int32)
    request_count = jnp.sum((wanted[:, :, None] == target[None, None, :]).astype(jnp.int32), axis=1)
    outgoing = jnp.einsum(
        "wr,rtkc->wtkc",
        request_count.astype(jnp.bfloat16),
        ref_cache,
        preferred_element_type=jnp.float32,
    ).astype(jnp.bfloat16)
    arrived = lax.all_to_all(outgoing, "wa", split_axis=0, concat_axis=0, tiled=True)
    picked = jnp.take(arrived, my_blocks // per_owner, axis=0)
    ref_keys = picked[:, :, 0].reshape(-1, channels)
    ref_values = picked[:, :, 1].reshape(-1, channels)
    head_outputs = []
    for head_index in range(head_count):
        first = head_index * HD
        head_query = query_flat[:, first : first + HD]
        scores = (
            jnp.einsum(
                "qc,kc->qk",
                head_query,
                key_flat[:, first : first + HD],
                preferred_element_type=jnp.float32,
            )
            * score_scale
        )
        scores = jnp.where(window, scores, -jnp.inf)
        row_max = jnp.max(scores, axis=1)
        ref_scores = (
            jnp.einsum(
                "qc,kc->qk",
                head_query,
                ref_keys[:, first : first + HD],
                preferred_element_type=jnp.float32,
            )
            * score_scale
        )
        ref_scores = jnp.where(flagged[:, None], ref_scores, -jnp.inf)
        row_max = jnp.maximum(row_max, jnp.max(ref_scores, axis=1))
        ref_probs = jnp.exp(ref_scores - row_max[:, None])
        ref_total = jnp.sum(ref_probs, axis=1)
        ref_part = jnp.dot(
            ref_probs.astype(jnp.bfloat16),
            ref_values[:, first : first + HD],
            preferred_element_type=jnp.float32,
        )
        probs = jnp.exp(scores - row_max[:, None])
        denominator = jnp.sum(probs, axis=1) + ref_total
        numerator = (
            jnp.dot(
                probs.astype(jnp.bfloat16),
                value_flat[:, first : first + HD],
                preferred_element_type=jnp.float32,
            )
            + ref_part
        )
        head_outputs.append(numerator / denominator[:, None])
    attended = jnp.concatenate(head_outputs, axis=1).astype(jnp.bfloat16)
    partial_term = jnp.dot(attended, proj_weight, preferred_element_type=jnp.float32).reshape(
        tile_rows, tile_cols, -1
    )
    return lax.psum_scatter(
        partial_term.astype(jnp.bfloat16), "head", scatter_dimension=2, tiled=True
    )


VMEM = pl.BlockSpec(memory_space=pltpu.VMEM)
SMEM = pl.BlockSpec(memory_space=pltpu.SMEM)
ANY = pl.BlockSpec(memory_space=pl.ANY)


def copied(pairs, sem):
    copies = [
        pltpu.make_async_copy(source, target, sem.at[n]) for n, (source, target) in enumerate(pairs)
    ]
    for copy in copies:
        copy.start()
    for copy in copies:
        copy.wait()


def attend_kernel(per_owner, tiles, count, me_ref, ids_ref, *refs):
    come, (qf_ref, own_ref, a_ref, b_ref, kf_ref) = refs[:tiles], refs[tiles : tiles + 5]
    o_refs, scratch = refs[tiles + 5 : 2 * tiles + 5], refs[2 * tiles + 5 :]
    s_ref, qr_ref, out_ref = scratch
    token_count = qf_ref.shape[1]
    head_rows = qr_ref.shape[1] // count
    block_tokens = (head_rows - token_count) // 2 // per_owner
    chosen_count = ids_ref.shape[1]
    factor = HD ** (-0.5) * math.log2(math.e)
    ones = jnp.ones((token_count, HD), jnp.bfloat16)
    ones_block = jnp.ones((block_tokens, HD), jnp.bfloat16)
    for k in range(tiles):
        qr_ref[me_ref[0] ^ k] = come[k][: qr_ref.shape[1]]

    def pieces(head, w):
        key_at = head * head_rows + token_count
        value_at = key_at + per_owner * block_tokens
        for other in range(max(w - 1, 0), min(w + 2, tiles)):
            for r, source in enumerate((a_ref, own_ref, b_ref)):
                yield (
                    functools.partial(lambda s, o: s[o, 2 * head], source, other),
                    functools.partial(lambda r, c: kf_ref[r, c], r, other - w + 1),
                    functools.partial(lambda s, o: s[o, 2 * head + 1], source, other),
                )
        for n in range(chosen_count):
            chosen = ids_ref[w, n]
            owner = lax.div(chosen, per_owner)
            start = pl.multiple_of(lax.rem(chosen, per_owner) * block_tokens, block_tokens)
            yield (
                functools.partial(lambda o, s: qr_ref[o, pl.ds(key_at + s, block_tokens)], owner, start),
                lambda: kf_ref[3, 0, :block_tokens],
                functools.partial(lambda o, s: qr_ref[o, pl.ds(value_at + s, block_tokens)], owner, start),
            )

    def score(head, w, slot):
        query_at = head * head_rows
        q_wide = jnp.concatenate(
            [qr_ref[w, query_at : query_at + token_count], qf_ref[w]], axis=1
        )
        at, best = 0, None
        for keys, features, _ in pieces(head, w):
            wide = jnp.concatenate([keys(), features()], axis=1)
            s = lax.dot_general(
                q_wide, wide, (((1,), (1,)), ((), ())), preferred_element_type=jnp.float32
            )
            s_ref[slot, :, at : at + s.shape[1]] = s
            at += s.shape[1]
            for part in range(0, s.shape[1], HD):
                piece = s[:, part : part + HD]
                best = piece if best is None else jnp.maximum(best, piece)
            yield None
        yield jnp.max(best, axis=1, keepdims=True)

    def weigh(head, w, slot, row_max):
        at = 0
        total = jnp.zeros((token_count, 2 * HD), jnp.float32)
        for _, _, values in pieces(head, w):
            v = values()
            width = v.shape[0]
            probs = jnp.exp2((s_ref[slot, :, at : at + width] - row_max) * factor)
            total = total + jnp.dot(
                probs.astype(jnp.bfloat16),
                jnp.concatenate([v, jnp.ones((width, HD), jnp.bfloat16)], axis=1),
                preferred_element_type=jnp.float32,
            )
            at += width
            yield None
        out_ref[w, head * token_count : (head + 1) * token_count] = (
            total[:, :HD] / total[:, HD:]
        ).astype(jnp.bfloat16)

    items = [(head, w) for head in range(count) for w in range(tiles)]
    row_max = None
    for n in range(len(items) + 1):
        first = score(*items[n], n % 2) if n < len(items) else iter(())
        second = weigh(*items[n - 1], 1 - n % 2, row_max) if n else iter(())
        running = [first, second]
        while running:
            for one in list(running):
                try:
                    got = next(one)
                    if got is not None:
                        row_max = got
                except StopIteration:
                    running.remove(one)
    for k in range(tiles):
        o_refs[k][...] = out_ref[me_ref[0] ^ k]


def attend(per_owner, me, ids, qr, q_features, own, first, second, k_features):
    tiles, token_count, _ = q_features.shape
    count = own.shape[1] // 2
    key_count = (9 + ids.shape[1]) * token_count
    rows = qr[0].shape[0] // 128 * 128
    return pl.pallas_call(
        functools.partial(attend_kernel, per_owner, tiles, count),
        out_shape=[jax.ShapeDtypeStruct((count * token_count, HD), jnp.bfloat16)] * tiles,
        in_specs=[SMEM] * 2 + [VMEM] * (tiles + 5),
        out_specs=[VMEM] * tiles,
        scratch_shapes=[
            pltpu.VMEM((2, token_count, key_count), jnp.float32),
            pltpu.VMEM((tiles, rows, HD), jnp.bfloat16),
            pltpu.VMEM((tiles, count * token_count, HD), jnp.bfloat16),
        ],
        compiler_params=pltpu.CompilerParams(vmem_limit_bytes=12 << 20),
        cost_estimate=pl.CostEstimate(
            flops=count * tiles * 4 * token_count * key_count * HD,
            transcendentals=count * tiles * token_count * key_count,
            bytes_accessed=3 * own.size * 2,
        ),
        name="attend",
    )(me, ids, *in_vmem(*qr, q_features, own, first, second, k_features))


def grid_lanes(tile_rows, tile_cols):
    token_count = tile_rows * tile_cols
    lane = lax.broadcasted_iota(jnp.int32, (token_count, HD), 1)
    token = lax.broadcasted_iota(jnp.int32, (token_count, HD), 0)
    row, col = lax.div(token, tile_cols), lax.rem(token, tile_cols)
    is_row = lane < tile_rows
    is_col = (lane >= tile_rows) & (lane < tile_rows + tile_cols)
    is_flag = lane == tile_rows + tile_cols
    return lane, row, col, is_row, is_col, is_flag


def query_features_kernel(tile_rows, tile_cols, me_ref, *refs):
    *come, o_ref = refs
    lane, row, col, is_row, is_col, is_flag = grid_lanes(tile_rows, tile_cols)
    hot = ((is_row & (lane == row)) | (is_col & (lane - tile_rows == col))).astype(jnp.float32)
    token = row * tile_cols + col
    for k, ref in enumerate(come):
        flags = ref[...].astype(jnp.float32)
        flag = jnp.zeros(hot.shape, jnp.float32)
        for part in range(tile_rows * tile_cols // HD):
            flag += jnp.where(token - part * HD == lane, flags[part : part + 1], 0.0)
        column = jnp.sum(flag, axis=1, keepdims=True)
        o_ref[me_ref[0] ^ k] = jnp.where(is_flag, 1.0 - column, hot).astype(jnp.bfloat16)


def query_features(tile_rows, tile_cols, me, come):
    tiles = len(come)
    last = come[0].shape[0] // 16 - 1
    return pl.pallas_call(
        functools.partial(query_features_kernel, tile_rows, tile_cols),
        grid=(1,),
        out_shape=jax.ShapeDtypeStruct((tiles, tile_rows * tile_cols, HD), jnp.bfloat16),
        in_specs=[SMEM] + [pl.BlockSpec((16, HD), lambda i: (last, 0))] * tiles,
        out_specs=VMEM,
        compiler_params=pltpu.CompilerParams(vmem_limit_bytes=4 << 20),
        name="query_features",
    )(me, *come)


def key_features_kernel(tile_rows, tile_cols, side_ref, o_ref):
    lane, row, col, is_row, is_col, is_flag = grid_lanes(tile_rows, tile_cols)
    far_rows = []
    for slot in range(2):
        toward, there = side_ref[slot, 0], side_ref[slot, 1]
        beyond = (row - lane) * toward > 0
        far_rows.append(jnp.where(is_row & (beyond | (there == 0)), FAR, 0.0))
    near = jnp.zeros_like(far_rows[0])
    far_rows = [far_rows[0], near, far_rows[1]]
    far_cols = [
        jnp.where(is_col & (col < lane - tile_rows), FAR, 0.0),
        near,
        jnp.where(is_col & (col > lane - tile_rows), FAR, 0.0),
    ]
    for r in range(3):
        for c in range(3):
            o_ref[r, c] = (far_rows[r] + far_cols[c]).astype(jnp.bfloat16)
    for c in range(3):
        o_ref[3, c] = jnp.where(is_flag, FAR, 0.0).astype(jnp.bfloat16)


def key_features(tile_rows, tile_cols, sides):
    return pl.pallas_call(
        functools.partial(key_features_kernel, tile_rows, tile_cols),
        out_shape=jax.ShapeDtypeStruct((4, 3, tile_rows * tile_cols, HD), jnp.bfloat16),
        in_specs=[SMEM],
        out_specs=VMEM,
        compiler_params=pltpu.CompilerParams(vmem_limit_bytes=4 << 20),
        name="key_features",
    )(sides)


def pack_kv_kernel(tiles, share, heads, me_ref, x_ref, *refs):
    *o_refs, sem = refs
    pairs = []
    for k, o_ref in enumerate(o_refs):
        for n, head in enumerate(heads):
            first = pl.multiple_of(((me_ref[0] ^ k) * share + head) * HD, HD)
            pairs.append((x_ref.at[:, :, pl.ds(first, HD)], o_ref.at[2 * n : 2 * n + 2]))
    copied(pairs, sem)


def pack_kv(me, x, heads, tiles, share):
    shape = jax.ShapeDtypeStruct((2 * len(heads), x.shape[1], HD), x.dtype)
    return pl.pallas_call(
        functools.partial(pack_kv_kernel, tiles, share, heads),
        out_shape=[shape] * tiles,
        in_specs=[SMEM, ANY],
        out_specs=[VMEM] * tiles,
        scratch_shapes=[pltpu.SemaphoreType.DMA((tiles * len(heads),))],
        compiler_params=pltpu.CompilerParams(vmem_limit_bytes=8 << 20),
        name="pack_kv",
    )(me, x)


def order_kernel(me_ref, *refs):
    *come, o_ref, sem = refs
    copied([(ref, o_ref.at[me_ref[0] ^ k]) for k, ref in enumerate(come)], sem)


def order(me, come):
    tiles = len(come)
    return pl.pallas_call(
        order_kernel,
        out_shape=jax.ShapeDtypeStruct((tiles, *come[0].shape), come[0].dtype),
        in_specs=[SMEM] + [ANY] * tiles,
        out_specs=VMEM,
        scratch_shapes=[pltpu.SemaphoreType.DMA((tiles,))],
        compiler_params=pltpu.CompilerParams(vmem_limit_bytes=6 << 20),
        name="order",
    )(me, *come)


def pack_qr_kernel(tiles, share, chunks, me_ref, q_ref, r_ref, f_ref, *refs):
    *o_refs, sem = refs
    token_count = q_ref.shape[0]
    block_tokens = r_ref.shape[1]
    pairs = []
    for c, heads in enumerate(chunks):
        for k in range(tiles):
            o_ref = o_refs[c * tiles + k]
            at = 0
            for head in heads:
                lanes = pl.ds(pl.multiple_of(((me_ref[0] ^ k) * share + head) * HD, HD), HD)
                pairs.append((q_ref.at[:, lanes], o_ref.at[at : at + token_count]))
                at += token_count
                for part in range(2):
                    pairs.append((r_ref.at[part, :, lanes], o_ref.at[at : at + block_tokens]))
                    at += block_tokens
            if f_ref.shape[0] + at == o_ref.shape[0]:
                pairs.append((f_ref, o_ref.at[at : at + f_ref.shape[0]]))
    copied(pairs, sem)


def pack_qr(me, q, r, f, chunks, tiles, share):
    rows = q.shape[0] + 2 * r.shape[1]
    shapes = [
        jax.ShapeDtypeStruct((rows * len(heads) + (f.shape[0] if heads[0] == 0 else 0), HD), q.dtype)
        for c, heads in enumerate(chunks)
        for k in range(tiles)
    ]
    flat = pl.pallas_call(
        functools.partial(pack_qr_kernel, tiles, share, chunks),
        out_shape=shapes,
        in_specs=[SMEM] + [ANY] * 3,
        out_specs=[VMEM] * len(shapes),
        scratch_shapes=[pltpu.SemaphoreType.DMA((tiles * (3 * share + 1),))],
        compiler_params=pltpu.CompilerParams(vmem_limit_bytes=8 << 20),
        name="pack_qr",
    )(me, q, r, f)
    return [flat[n * tiles : (n + 1) * tiles] for n in range(len(chunks))]


def fetch_rows(tiles, share, chunk, me_ref, w_hbm, w_ref, sem):
    depth = len(chunk) * HD
    copies = []
    for k in range(tiles):
        first = pl.multiple_of(((me_ref[0] ^ k) * share + chunk[0]) * HD, HD)
        copies.append(
            pltpu.make_async_copy(
                w_hbm.at[pl.ds(first, depth)], w_ref.at[k], sem.at[k]
            )
        )
        copies[-1].start()
    return copies


def side_by_side(ref, count):
    token_count = ref.shape[0] // count
    return jnp.concatenate(
        [ref[n * token_count : (n + 1) * token_count] for n in range(count)], axis=1
    )


def project_early_kernel(tiles, share, chunks, me_ref, w_hbm, *refs):
    *heads, o_ref, late_ref, w_ref, sem, late_sem = refs
    width = o_ref.shape[2]
    chunk = chunks[0]
    copies = fetch_rows(tiles, share, chunk, me_ref, w_hbm, w_ref, sem)
    late = fetch_rows(tiles, share, chunks[1], me_ref, w_hbm, late_ref, late_sem)
    for k in range(tiles):
        copies[k].wait()
        x = side_by_side(heads[k], len(chunk))
        for half in range(2):
            part = jnp.dot(
                x, w_ref[k, :, half * width : (half + 1) * width], preferred_element_type=jnp.float32
            )
            o_ref[half] = part if k == 0 else o_ref[half] + part
    for copy in late:
        copy.wait()


def project_early(me, weight, heads, chunks, share):
    chunk = chunks[0]
    tiles = len(heads)
    token_count = heads[0].shape[0] // len(chunk)
    width = weight.shape[1]
    return pl.pallas_call(
        functools.partial(project_early_kernel, tiles, share, chunks),
        out_shape=[
            jax.ShapeDtypeStruct((2, token_count, width // 2), jnp.float32),
            jax.ShapeDtypeStruct((tiles, len(chunks[1]) * HD, width), weight.dtype),
        ],
        in_specs=[SMEM, ANY] + [VMEM] * tiles,
        out_specs=[VMEM] * 2,
        scratch_shapes=[
            pltpu.VMEM((tiles, len(chunk) * HD, width), jnp.bfloat16),
            pltpu.SemaphoreType.DMA((tiles,)),
            pltpu.SemaphoreType.DMA((tiles,)),
        ],
        compiler_params=pltpu.CompilerParams(vmem_limit_bytes=18 << 20),
        name="project_early",
    )(me, pltpu.with_memory_space_constraint(weight, pltpu.HBM), *heads)


def project_kernel(tiles, count, which_ref, w_ref, early_ref, *refs):
    *heads, o_ref = refs
    width = o_ref.shape[1]
    columns = pl.ds(pl.multiple_of(which_ref[0] * width, HD), width)
    total = early_ref[which_ref[0]]
    for k in range(tiles):
        total = total + jnp.dot(
            side_by_side(heads[k], count), w_ref[k, :, columns], preferred_element_type=jnp.float32
        )
    o_ref[...] = total.astype(o_ref.dtype)


def project(which, weight, early, heads, count):
    tiles = len(heads)
    _, token_count, width = early.shape
    return pl.pallas_call(
        functools.partial(project_kernel, tiles, count),
        out_shape=jax.ShapeDtypeStruct((token_count, width), jnp.bfloat16),
        in_specs=[SMEM] + [VMEM] * (2 + tiles),
        out_specs=VMEM,
        compiler_params=pltpu.CompilerParams(vmem_limit_bytes=10 << 20),
        name="project",
    )(which.reshape(1), weight, early, *heads)


def in_vmem(*arrays):
    return [pltpu.with_memory_space_constraint(x, pltpu.VMEM) for x in arrays]


def after(x, *others):
    return lax.optimization_barrier((x, *others))[0]


def by_head(queries, keys_values, ref_cache, ref_ids, flags, proj_weight):
    tile_rows, tile_cols, channels = queries.shape
    tiles = lax.axis_size("wa")
    token_count = tile_rows * tile_cols
    share = channels // HD // tiles
    chunks = [list(range(share - 1)), [share - 1]]
    per_owner = ref_cache.shape[0]
    heights = lax.axis_size("ha")
    kv = keys_values.reshape(token_count, 2, channels).transpose(1, 0, 2)

    def swap(come):
        return [
            x if k == 0 else lax.ppermute(x, "wa", [(i, i ^ k) for i in range(tiles)])
            for k, x in enumerate(come)
        ]

    even = [(i, i + 1) for i in range(0, heights - 1, 2)]
    odd = [(i, i + 1) for i in range(1, heights - 1, 2)]
    both_ways = [[(b, a) for a, b in pairs] + pairs for pairs in (even, odd)]

    def neighbours(x):
        return [lax.ppermute(x, "ha", pairs) for pairs in both_ways]

    place = lax.axis_index("ha")
    toward = 1 - 2 * (place % 2)
    sides = jnp.stack(
        [
            jnp.stack([way, ((place + way >= 0) & (place + way < heights)).astype(jnp.int32)])
            for way in (toward, -toward)
        ]
    )
    me = lax.axis_index("wa").reshape(1)
    packed = [pack_kv(me, kv, chunks[0], tiles, share)]
    for chunk in chunks[1:]:
        packed.append(pack_kv(me, after(kv, *packed[-1]), chunk, tiles, share))
    come = [swap(packed[0])]
    for pieces in packed[1:]:
        come.append(swap([after(x, *come[-1][1:]) for x in pieces]))
    own = [order(me, lax.optimization_barrier((*come[0], *packed[-1]))[:tiles])]
    around = [neighbours(own[0])]
    late_q, late_r = lax.optimization_barrier((queries, ref_cache, packed[-1][1]))[:2]
    late_r = late_r.reshape(-1, 2, channels).transpose(1, 0, 2)
    flag_rows = jnp.pad(flags.reshape(-1, HD), ((0, 16 - token_count // HD), (0, 0)))
    late_q = late_q.reshape(token_count, channels)
    flag_rows = flag_rows.astype(jnp.bfloat16)
    qr = pack_qr(me, late_q, late_r, flag_rows, chunks[:1], tiles, share)
    later = lax.optimization_barrier((late_q, late_r, flag_rows, come[-1][1]))[:3]
    qr += pack_qr(me, *later, chunks[1:], tiles, share)
    k_features = key_features(tile_rows, tile_cols, sides)
    for pieces in come[1:]:
        own.append(order(me, lax.optimization_barrier((*pieces, qr[0][1], k_features))[:tiles]))
        around.append(neighbours(after(own[-1], *around[-1])))
    arrived = []
    for n, pieces in enumerate(qr):
        gates = come[-1] if n == 0 else arrived[-1]
        arrived.append(swap([after(x, gates[max(k, 1)]) if k else x for k, x in enumerate(pieces)]))
    q_features = query_features(tile_rows, tile_cols, me, arrived[0])
    heads = [
        swap(
            attend(
                per_owner, me, ref_ids[0], arrived[n], q_features, own[n], *around[n], k_features
            )
        )
        for n in range(len(chunks))
    ]
    early, weight = project_early(me, proj_weight, heads[0], chunks, share)
    mine = lax.axis_index("head")
    theirs = project(1 - mine, weight, early, heads[1], len(chunks[1]))
    got = lax.ppermute(theirs, "head", [(0, 1), (1, 0)])
    own_part = project(mine, weight, early, heads[1], len(chunks[1]))
    total = own_part.astype(jnp.float32) + got.astype(jnp.float32)
    return total.astype(jnp.bfloat16).reshape(tile_rows, tile_cols, -1)


def on_device(queries, *others):
    head_count = queries.shape[2] // HD
    fits = (
        head_count % lax.axis_size("wa") == 0
        and lax.axis_size("wa") & (lax.axis_size("wa") - 1) == 0
        and head_count // lax.axis_size("wa") > 1
        and lax.axis_size("head") == 2
        and queries.shape[0] == RADIUS
        and queries.shape[1] == RADIUS
    )
    return (by_head if fits else by_tile)(queries, *others)


def solution(mesh):
    return jax.shard_map(
        on_device,
        mesh=mesh,
        in_specs=(
            P("ha", "wa", "head"),
            P("ha", "wa", None, "head"),
            P("wa", None, None, "head"),
            P("ha", None, None),
            P("ha", "wa"),
            P("head", None),
        ),
        out_specs=P("ha", "wa", "head"),
        check_vma=False,
    )
```
